32 devices in a mesh: clip: 4 (over x, core), seq: 8 (over z, y).
Axes of the slice: x: 2, y: 2, z: 4, core: 2. Of those that a mesh axis runs over, the one named last changes fastest.
Arguments:
- video_query: bfloat16 [4096, 4096], P(('clip', 'seq')), parts along dimension 0
- video_key: bfloat16 [4096, 4096], P(('clip', 'seq')), parts along dimension 0
- video_value: bfloat16 [4096, 4096], P(('clip', 'seq')), parts along dimension 0, may hold values from -6 to 6
- cross_query: bfloat16 [4096, 4096], P(('clip', 'seq')), parts along dimension 0
- text_rows: bfloat16 [2048, 4096], P(('clip', 'seq')), parts along dimension 0, may hold values from -6 to 6
- text_block: int32 [32], P('clip'), parts along dimension 0, may hold values from 0 to 7, each once
- text_length: int32 [4], P('clip'), parts along dimension 0, may hold values from 64 to 512
- key_weight: bfloat16 [4096, 4096], P(None, 'seq'), may hold values from -0.09375 to 0.09375
- value_weight: bfloat16 [4096, 4096], P(None, 'seq'), may hold values from -0.09375 to 0.09375
Outputs:
- self_out: bfloat16 [4096, 4096], P(('clip', 'seq')), parts along dimension 0
- cross_out: bfloat16 [4096, 4096], P(('clip', 'seq')), parts along dimension 0
The draws below stay inside these ranges and needn't reach their ends.
There are 4 independent parts, one for each index of `clip`. The reference program is written for one: setup_inputs(seed, part) draws one part's arguments, and reference() takes and returns one part's arrays. A program takes and returns all parts, laid end to end along the dimension named above; an argument that names none is the same for every part. Nothing has to cross between parts.
Inputs may be any that keep to these rules, and one draw needn't show every extreme that they name: A permutation: arrival block j holds prompt rows text_block[j] * 64 onward.
All inputs are finite; a program needn't handle non-finite values.
Results may differ from the reference program's by a relative error of at most 0.012.
The reference program's roundings to bfloat16 on the way count: a program that leaves them out, or rounds other values in their place, can miss the bound.
Values may be sent and summed in bfloat16 or wider, within the bound.
A program may use at most 128 MiB of HBM per device.

```python
import jax
import jax.numpy as jnp
from jax import lax

D_TEXT = 4096
HEAD_DIM = 128
TEXT = 512
INNER = 4096
TOKENS = 1024
TXT_DEV = 64
N_SEQ = 8


def drawn_pair(key):
    key_seed = jax.random.fold_in(key, 11)
    query_seed = jax.random.fold_in(key, 12)
    key_rows = jnp.clip(jax.random.normal(key_seed, (TOKENS, INNER), jnp.float32), -6.0, 6.0)
    base = jnp.clip(jax.random.normal(query_seed, (TOKENS, INNER), jnp.float32), -6.0, 6.0) * 2.5
    queries = base
    return (queries, key_rows)


def draw_video_query(key, part):
    queries, key_rows = drawn_pair(key)
    return queries.astype(jnp.bfloat16)


def draw_video_key(key, part):
    queries, key_rows = drawn_pair(key)
    return key_rows.astype(jnp.bfloat16)


def draw_cross_query(key, part):
    base_seed = jax.random.fold_in(key, 21)
    base = jnp.clip(jax.random.normal(base_seed, (TOKENS, INNER), jnp.float32), -6.0, 6.0) * 2.5
    return base.astype(jnp.bfloat16)


def draw_text_length(key, part):
    drawn = jax.random.randint(jax.random.fold_in(key, 31), (1,), TEXT // 8, TEXT + 1)
    coin = jax.random.randint(jax.random.fold_in(key, 32), (1,), 0, 4)
    full_value = jnp.full((1,), TEXT, dtype=jnp.int32)
    return jnp.where(coin == 0, full_value, drawn).astype(jnp.int32)


def block_scale(stream_key, extent, cuts, low, largest):
    def one(axis_at, shards_of):
        heights = jax.random.uniform(jax.random.fold_in(jax.random.fold_in(stream_key, 6), axis_at), (shards_of,), jnp.float32, low / len(cuts), largest / len(cuts))
        return jnp.repeat(jnp.exp(heights), extent[axis_at] // shards_of).reshape((-1,) + (1,) * (len(extent) - axis_at - 1))

    loudness = one(*cuts[0])
    for cut in cuts[1:]:
        loudness = loudness * one(*cut)
    return loudness


def normal_values(key, extent, spread, bound, split=(), kind=jnp.bfloat16):
    entries = spread * jax.random.normal(key, extent, jnp.float32)
    if split:
        entries = entries * block_scale(key, extent, split, -0.22, 0.18)
    return jnp.clip(entries, -bound, bound).astype(kind)


def setup_inputs(seed: int = 0, part: int = 0) -> dict:
    splits = jax.random.split(jax.random.key(seed), 10)
    part_keys = jax.random.split(jax.random.fold_in(splits[9], part), 10)
    return {
        "video_query": draw_video_query(jax.random.fold_in(jax.random.fold_in(splits[9], part), 71), part),
        "video_key": draw_video_key(jax.random.fold_in(jax.random.fold_in(splits[9], part), 71), part),
        "video_value": normal_values(part_keys[2], (TOKENS, INNER), 1.0, 6.0, ((0, 8),)),
        "cross_query": draw_cross_query(jax.random.fold_in(jax.random.fold_in(splits[9], part), 71), part),
        "text_rows": normal_values(part_keys[4], (TEXT, D_TEXT), 1.0, 6.0, ((0, 8),)),
        "text_block": jax.random.permutation(part_keys[5], N_SEQ).astype(jnp.int32),
        "text_length": draw_text_length(jax.random.fold_in(jax.random.fold_in(splits[9], part), 71), part),
        "key_weight": normal_values(splits[7], (D_TEXT, INNER), D_TEXT ** -0.5, 0.09375, ((1, 8),)),
        "value_weight": normal_values(splits[8], (D_TEXT, INNER), D_TEXT ** -0.5, 0.09375, ((1, 8),)),
    }


def attend(queries, key_rows, value_rows, key_valid):
    query_count = queries.shape[0]
    key_count = key_rows.shape[0]
    head_count = queries.shape[1] // HEAD_DIM
    score_scale = HEAD_DIM ** -0.5
    query_heads = queries.reshape(query_count, head_count, HEAD_DIM).transpose(1, 0, 2)
    key_heads = key_rows.reshape(key_count, head_count, HEAD_DIM).transpose(1, 0, 2)
    value_heads = value_rows.reshape(key_count, head_count, HEAD_DIM).transpose(1, 0, 2)

    def one_head(operands):
        head_query, head_key, head_value = operands
        scores = jnp.dot(head_query, head_key.T, preferred_element_type=jnp.float32) * score_scale
        if key_valid is not None:
            scores = jnp.where(key_valid[None, :], scores, -jnp.inf)
        highest = jnp.max(scores, axis=-1, keepdims=True)
        exponent = jnp.exp(scores - highest)
        weights = (exponent / jnp.sum(exponent, axis=-1, keepdims=True)).astype(jnp.bfloat16)
        return jnp.dot(weights, head_value, preferred_element_type=jnp.float32).astype(jnp.bfloat16)

    outputs = lax.map(one_head, (query_heads, key_heads, value_heads))
    return outputs.transpose(1, 0, 2).reshape(query_count, head_count * HEAD_DIM)


def reference(video_query, video_key, video_value, cross_query, text_rows, text_block, text_length, key_weight, value_weight):
    text_keys = jnp.dot(text_rows, key_weight, preferred_element_type=jnp.float32).astype(jnp.bfloat16)
    text_values = jnp.dot(text_rows, value_weight, preferred_element_type=jnp.float32).astype(jnp.bfloat16)
    arrival = jnp.arange(TEXT, dtype=jnp.int32)
    owners = arrival // TXT_DEV
    blocks_held = text_block[owners].astype(jnp.int32)
    key_valid = blocks_held * TXT_DEV + arrival % TXT_DEV < text_length[0]
    self_out = attend(video_query, video_key, video_value, None)
    cross_out = attend(cross_query, text_keys, text_values, key_valid)
    return self_out, cross_out
```

```python
import functools
import math

import jax
import jax.numpy as jnp
from jax import lax
from jax.experimental import pallas as pl
from jax.experimental.pallas import tpu as pltpu
from jax.sharding import PartitionSpec as P

HEAD_DIM = 128
MESH = pl.DeviceIdType.MESH
F32 = jnp.float32
BF16 = jnp.bfloat16
SCORE_SCALE = HEAD_DIM ** (-0.5) * math.log2(math.e)


def softmax_rows(scores, bias):
    scores = scores * SCORE_SCALE
    if bias is not None:
        scores = scores + bias
    highest = jnp.max(scores, axis=-1, keepdims=True)
    exponent = jnp.exp2(scores - highest)
    total = jnp.sum(exponent, axis=-1, keepdims=True)
    return (exponent * (1.0 / total)).astype(BF16)


def attend(query, key, value, bias, out, block):
    def one(step, carry):
        rows = pl.ds(pl.multiple_of(step * block, block), block)
        scores = lax.dot_general(
            query[rows, :], key[...], (((1,), (1,)), ((), ())), preferred_element_type=F32
        )
        weights = softmax_rows(scores, None if bias is None else bias[...])
        out[rows, :] = jnp.dot(weights, value[...], preferred_element_type=F32).astype(BF16)
        return carry

    lax.fori_loop(0, query.shape[0] // block, one, 0)


def kernel(
    n,
    lines,
    block_in,
    length_in,
    q_in,
    k_in,
    v_in,
    c_in,
    text_in,
    wk_in,
    wv_in,
    self_out,
    cross_out,
    q_buf,
    k_buf,
    v_buf,
    c_buf,
    so_buf,
    co_buf,
    text,
    wk,
    wv,
    tk,
    tv,
    bias,
    block_ref,
    length_ref,
    in_send,
    in_recv,
    out_send,
    out_recv,
    text_recv,
    up_send,
    down_send,
    side_send,
    w_sem,
    small_sem,
    ready,
):
    heads, tokens, dim = q_buf.shape
    own = tokens // n
    shard = text.shape[1]
    me = lax.axis_index("seq")
    side = n // lines
    pos = me // side
    lane = me % side

    def to(target):
        return {"seq": target}

    barrier = pltpu.get_barrier_semaphore()

    w_copies = [
        pltpu.make_async_copy(wk_in, wk, w_sem.at[0]),
        pltpu.make_async_copy(wv_in, wv, w_sem.at[1]),
    ]
    small_copies = [
        pltpu.make_async_copy(block_in, block_ref, small_sem.at[0]),
        pltpu.make_async_copy(length_in, length_ref, small_sem.at[1]),
    ]
    own_text = pltpu.make_async_copy(text_in, text.at[me], text_recv.at[me])
    own_text.start()

    low = lines // 2 - 1
    high = low + 1
    middle = jnp.logical_or(pos == low, pos == high)
    outer_lines = [line for line in range(lines) if line not in (low, high)]

    def text_send(source, index, target, sem):
        return pltpu.make_async_remote_copy(
            src_ref=source,
            dst_ref=text.at[index],
            send_sem=sem,
            recv_sem=text_recv.at[index],
            device_id=to(target),
            device_id_type=MESH,
        )

    def forward_up(source, line, step):
        copy = text_send(source, line * side + lane, me + side, up_send.at[step])

        @pl.when(pos + 1 < lines)
        def _():
            copy.start()

    def forward_down(source, line, step):
        copy = text_send(source, line * side + lane, me - side, down_send.at[step])

        @pl.when(pos >= 1)
        def _():
            copy.start()

    def forward_side(source, line):
        index = line * side + lane
        for k in range(1, side):
            text_send(
                source, index, pos * side + (lane + k) % side, side_send.at[line, k]
            ).start()

    def text_wait(index):
        pltpu.make_async_copy(text.at[index], text.at[index], text_recv.at[index]).wait()

    def relay(step):
        @pl.when(pos >= step)
        def _():
            index = (pos - step) * side + lane
            text_wait(index)
            forward_up(text.at[index], pos - step, step)
            forward_side(text.at[index], pos - step)

        @pl.when(pos + step < lines)
        def _():
            index = (pos + step) * side + lane
            text_wait(index)
            forward_down(text.at[index], pos + step, step)
            forward_side(text.at[index], pos + step)

    arrays = ((q_in, q_buf), (k_in, k_buf), (v_in, v_buf), (c_in, c_buf))

    def columns(owner, h):
        return pl.ds(pl.multiple_of((owner * heads + h) * dim, dim), dim)

    def rows(owner):
        return pl.ds(pl.multiple_of(owner * own, own), own)

    def send_in(which, h):
        def one(d, carry):
            target = (me + d) % n
            for t in which:
                source, landing = arrays[t]
                pltpu.make_async_remote_copy(
                    src_ref=source.at[:, columns(target, h)],
                    dst_ref=landing.at[h, rows(me), :],
                    send_sem=in_send.at[t, h],
                    recv_sem=in_recv.at[t, h],
                    device_id=to(target),
                    device_id_type=MESH,
                ).start()
            return carry

        for t in which:
            source, landing = arrays[t]
            pltpu.make_async_copy(
                source.at[:, columns(me, h)], landing.at[h, rows(me), :], in_recv.at[t, h]
            ).start()
        lax.fori_loop(1, n, one, 0)

    def wait_in(which, h):
        for t in which:
            landing = arrays[t][1].at[h]
            pltpu.make_async_copy(landing, landing, in_recv.at[t, h]).wait()

    results = ((so_buf, self_out), (co_buf, cross_out))

    def send_out(t, h):
        source, landing = results[t]

        def one(d, carry):
            target = (me + d) % n
            pltpu.make_async_remote_copy(
                src_ref=source.at[h, rows(target), :],
                dst_ref=landing.at[:, columns(me, h)],
                send_sem=out_send.at[t, h],
                recv_sem=out_recv.at[t],
                device_id=to(target),
                device_id_type=MESH,
            ).start()
            return carry

        lax.fori_loop(1, n, one, 0)
        pltpu.make_async_copy(
            source.at[h, rows(me), :], landing.at[:, columns(me, h)], out_recv.at[t]
        ).start()

    block = math.gcd(tokens, 256)

    def self_head(h):
        wait_in((0, 1, 2), h)
        attend(q_buf.at[h], k_buf.at[h], v_buf.at[h], None, so_buf.at[h], block)
        send_out(0, h)

    def hail(sem, line, lane_of):
        pl.semaphore_signal(
            sem, inc=1, device_id=to(line * side + lane_of), device_id_type=MESH
        )

    @pl.when(middle)
    def _():
        hail(barrier, low + high - pos, lane)
        pl.semaphore_wait(barrier, 1)

        @pl.when(pos == low)
        def _():
            forward_up(text_in, pos, 0)

        @pl.when(pos == high)
        def _():
            forward_down(text_in, pos, 0)

        for line in outer_lines:
            for k in range(side):
                hail(barrier, line, k)
        pl.semaphore_wait(barrier, len(outer_lines) * side)

        @pl.when(pos == low)
        def _():
            for line in outer_lines:
                if line < low:
                    hail(ready, line, lane)
            forward_down(text_in, pos, 0)

        @pl.when(pos == high)
        def _():
            for line in outer_lines:
                if line > high:
                    hail(ready, line, lane)
            forward_up(text_in, pos, 0)

    @pl.when(jnp.logical_not(middle))
    def _():
        pl.semaphore_wait(barrier, 2 * side)
        for line in (low, high):
            for k in range(side):
                hail(barrier, line, k)
        pl.semaphore_wait(ready, 1)
        forward_up(text_in, pos, 0)
        forward_down(text_in, pos, 0)

    forward_side(text_in, pos)
    send_in((0, 1, 2), 0)
    for copy in w_copies + small_copies:
        copy.start()
    for step in range(1, max(lines, heads)):
        if step < lines:
            relay(step)
        if step < heads:
            send_in((0, 1, 2), step)
        if step == lines - 1 or (step == heads - 1 and heads > lines):
            for h in range(heads):
                send_in((3,), h)
        if step <= heads:
            self_head(step - 1)
    for h in range(max(lines, heads) - 1, heads):
        self_head(h)

    text_wait(me)
    for line in range(lines):
        for k in range(1, side):
            text_wait(line * side + (lane + k) % side)
    for copy in w_copies + small_copies:
        copy.wait()

    text_rows = n * shard
    flat = text.reshape(text_rows, text.shape[2])
    tall = math.gcd(text_rows, 256)
    wide = math.gcd(wk.shape[1], 256)
    across = wk.shape[1] // wide

    def project(step, carry):
        r = pl.ds(pl.multiple_of((step // across) * tall, tall), tall)
        c = pl.ds(pl.multiple_of((step % across) * wide, wide), wide)
        tk[r, c] = jnp.dot(flat[r, :], wk[:, c], preferred_element_type=F32).astype(BF16)
        tv[r, c] = jnp.dot(flat[r, :], wv[:, c], preferred_element_type=F32).astype(BF16)
        return carry

    lax.fori_loop(0, (text_rows // tall) * across, project, 0)

    arrival = lax.broadcasted_iota(jnp.int32, bias.shape, 1)
    limit = jnp.zeros(bias.shape, jnp.int32)
    for j in range(n):
        held = length_ref[0] - block_ref[j] * shard
        limit = jnp.where(arrival // shard == j, held, limit)
    bias[...] = jnp.where(arrival % shard < limit, 0.0, -jnp.inf).astype(F32)

    for h in range(heads):
        c = slice(h * dim, (h + 1) * dim)
        wait_in((3,), h)
        attend(c_buf.at[h], tk.at[:, c], tv.at[:, c], bias, co_buf.at[h], block)
        send_out(1, h)

    for t in range(4):
        landing = arrays[t][1]
        for h in range(heads):
            part = landing.at[h, pl.ds(0, (n - 1) * own), :]
            pltpu.make_async_copy(part, part, in_send.at[t, h]).wait()
    for t in range(2):
        source, landing = results[t]
        for h in range(heads):
            part = source.at[h, pl.ds(0, (n - 1) * own), :]
            pltpu.make_async_copy(part, part, out_send.at[t, h]).wait()
        pltpu.make_async_copy(landing, landing, out_recv.at[t]).wait()

    for step in range(lines):
        up = text_send(text_in, me, me, up_send.at[step])
        down = text_send(text_in, me, me, down_send.at[step])

        @pl.when(jnp.logical_and(pos + 1 < lines, pos >= step))
        def _():
            up.wait_send()

        @pl.when(jnp.logical_and(pos >= 1, pos + step < lines))
        def _():
            down.wait_send()

        for k in range(1, side):
            text_send(text_in, me, me, side_send.at[step, k]).wait_send()


def settle_kernel(a, b, a_out, b_out, sem):
    copies = [
        pltpu.make_async_copy(a, a_out, sem.at[0]),
        pltpu.make_async_copy(b, b_out, sem.at[1]),
    ]
    for copy in copies:
        copy.start()
    for copy in copies:
        copy.wait()


def settle(pair):
    any_spec = pl.BlockSpec(memory_space=pl.ANY)
    return tuple(
        pl.pallas_call(
            settle_kernel,
            name="settle",
            out_shape=[pltpu.HBM(x.shape, x.dtype) for x in pair],
            in_specs=[any_spec] * 2,
            out_specs=[any_spec] * 2,
            scratch_shapes=[pltpu.SemaphoreType.DMA((2,))],
            compiler_params=pltpu.CompilerParams(vmem_limit_bytes=1024 * 1024),
        )(*pair)
    )


def body(
    video_query,
    video_key,
    video_value,
    cross_query,
    text_rows,
    text_block,
    text_length,
    key_weight,
    value_weight,
):
    n = lax.axis_size("seq")
    lines = 4 if n % 4 == 0 else n
    own, inner = video_query.shape
    shard, d_text = text_rows.shape
    width = key_weight.shape[1]
    heads = width // HEAD_DIM
    tokens = own * n
    any_spec = pl.BlockSpec(memory_space=pl.ANY)
    head_buf = pltpu.VMEM((heads, tokens, HEAD_DIM), BF16)
    dma = pltpu.SemaphoreType.DMA
    return settle(
        pl.pallas_call(
            functools.partial(kernel, n, lines),
            name="video_block",
            out_shape=[pltpu.VMEM((own, inner), BF16)] * 2,
            in_specs=[any_spec] * 9,
            out_specs=[any_spec] * 2,
            scratch_shapes=[head_buf] * 6
            + [
                pltpu.VMEM((n, shard, d_text), BF16),
                pltpu.VMEM((d_text, width), BF16),
                pltpu.VMEM((d_text, width), BF16),
                pltpu.VMEM((n * shard, width), BF16),
                pltpu.VMEM((n * shard, width), BF16),
                pltpu.VMEM((1, n * shard), F32),
                pltpu.SMEM((n,), jnp.int32),
                pltpu.SMEM((1,), jnp.int32),
                dma((4, heads)),
                dma((4, heads)),
                dma((2, heads)),
                dma((2,)),
                dma((n,)),
                dma((lines,)),
                dma((lines,)),
                dma((lines, max(n // lines, 2))),
                dma((2,)),
                dma((2,)),
                pltpu.SemaphoreType.REGULAR,
            ],
            compiler_params=pltpu.CompilerParams(
                collective_id=0, has_side_effects=True, vmem_limit_bytes=58 * 1024 * 1024
            ),
        )(
            text_block,
            text_length,
            video_query,
            video_key,
            video_value,
            cross_query,
            text_rows,
            key_weight,
            value_weight,
        )
    )


def solution(mesh):
    return jax.shard_map(
        body,
        mesh=mesh,
        in_specs=(
            P(("clip", "seq"), None),
            P(("clip", "seq"), None),
            P(("clip", "seq"), None),
            P(("clip", "seq"), None),
            P(("clip", "seq"), None),
            P("clip"),
            P("clip"),
            P(None, "seq"),
            P(None, "seq"),
        ),
        out_specs=(P(("clip", "seq"), None), P(("clip", "seq"), None)),
        check_vma=False,
    )
```

```python
import functools
import math

import jax
import jax.numpy as jnp
from jax import lax
from jax.experimental import pallas as pl
from jax.experimental.pallas import tpu as pltpu
from jax.sharding import PartitionSpec as P

HEAD_DIM = 128
MESH = pl.DeviceIdType.MESH
F32 = jnp.float32
BF16 = jnp.bfloat16
SCORE_SCALE = HEAD_DIM ** (-0.5) * math.log2(math.e)


def softmax_rows(scores, bias):
    scores = scores * SCORE_SCALE
    if bias is not None:
        scores = scores + bias
    highest = jnp.max(scores, axis=-1, keepdims=True)
    exponent = jnp.exp2(scores - highest)
    total = jnp.sum(exponent, axis=-1, keepdims=True)
    return (exponent * (1.0 / total)).astype(BF16)


def attend(query, key, value, bias, out, block):
    def one(step, carry):
        rows = pl.ds(pl.multiple_of(step * block, block), block)
        scores = lax.dot_general(
            query[rows, :], key[...], (((1,), (1,)), ((), ())), preferred_element_type=F32
        )
        weights = softmax_rows(scores, None if bias is None else bias[...])
        out[rows, :] = jnp.dot(weights, value[...], preferred_element_type=F32).astype(BF16)
        return carry

    lax.fori_loop(0, query.shape[0] // block, one, 0)


def kernel(
    n,
    lines,
    block_in,
    length_in,
    q_in,
    k_in,
    v_in,
    c_in,
    text_in,
    wk_in,
    wv_in,
    self_out,
    cross_out,
    q_buf,
    k_buf,
    v_buf,
    c_buf,
    so_buf,
    co_buf,
    text,
    wk,
    wv,
    tk,
    tv,
    bias,
    block_ref,
    length_ref,
    in_send,
    in_recv,
    out_send,
    out_recv,
    text_recv,
    up_send,
    down_send,
    side_send,
    w_sem,
    small_sem,
    ready,
):
    heads, tokens, dim = q_buf.shape
    own = tokens // n
    shard = text.shape[1]
    me = lax.axis_index("seq")
    side = n // lines
    pos = me // side
    lane = me % side

    def to(target):
        return {"seq": target}

    barrier = pltpu.get_barrier_semaphore()

    w_copies = [
        pltpu.make_async_copy(wk_in, wk, w_sem.at[0]),
        pltpu.make_async_copy(wv_in, wv, w_sem.at[1]),
    ]
    small_copies = [
        pltpu.make_async_copy(block_in, block_ref, small_sem.at[0]),
        pltpu.make_async_copy(length_in, length_ref, small_sem.at[1]),
    ]
    own_text = pltpu.make_async_copy(text_in, text.at[me], text_recv.at[me])
    own_text.start()

    low = lines // 2 - 1
    high = low + 1
    middle = jnp.logical_or(pos == low, pos == high)
    outer_lines = [line for line in range(lines) if line not in (low, high)]

    def text_send(source, index, target, sem):
        return pltpu.make_async_remote_copy(
            src_ref=source,
            dst_ref=text.at[index],
            send_sem=sem,
            recv_sem=text_recv.at[index],
            device_id=to(target),
            device_id_type=MESH,
        )

    def forward_up(source, line, step):
        copy = text_send(source, line * side + lane, me + side, up_send.at[step])

        @pl.when(pos + 1 < lines)
        def _():
            copy.start()

    def forward_down(source, line, step):
        copy = text_send(source, line * side + lane, me - side, down_send.at[step])

        @pl.when(pos >= 1)
        def _():
            copy.start()

    def forward_side(source, line):
        index = line * side + lane
        for k in range(1, side):
            text_send(
                source, index, pos * side + (lane + k) % side, side_send.at[line, k]
            ).start()

    def text_wait(index):
        pltpu.make_async_copy(text.at[index], text.at[index], text_recv.at[index]).wait()

    def relay(step):
        @pl.when(pos >= step)
        def _():
            index = (pos - step) * side + lane
            text_wait(index)
            forward_up(text.at[index], pos - step, step)
            forward_side(text.at[index], pos - step)

        @pl.when(pos + step < lines)
        def _():
            index = (pos + step) * side + lane
            text_wait(index)
            forward_down(text.at[index], pos + step, step)
            forward_side(text.at[index], pos + step)

    arrays = ((q_in, q_buf), (k_in, k_buf), (v_in, v_buf), (c_in, c_buf))

    def columns(owner, h):
        return pl.ds(pl.multiple_of((owner * heads + h) * dim, dim), dim)

    def rows(owner):
        return pl.ds(pl.multiple_of(owner * own, own), own)

    def send_in(which, h):
        def one(d, carry):
            target = (me + d) % n
            for t in which:
                source, landing = arrays[t]
                pltpu.make_async_remote_copy(
                    src_ref=source.at[:, columns(target, h)],
                    dst_ref=landing.at[h, rows(me), :],
                    send_sem=in_send.at[t, h],
                    recv_sem=in_recv.at[t, h],
                    device_id=to(target),
                    device_id_type=MESH,
                ).start()
            return carry

        for t in which:
            source, landing = arrays[t]
            pltpu.make_async_copy(
                source.at[:, columns(me, h)], landing.at[h, rows(me), :], in_recv.at[t, h]
            ).start()
        lax.fori_loop(1, n, one, 0)

    def wait_in(which, h):
        for t in which:
            landing = arrays[t][1].at[h]
            pltpu.make_async_copy(landing, landing, in_recv.at[t, h]).wait()

    results = ((so_buf, self_out), (co_buf, cross_out))

    def send_out(t, h, parity):
        source, landing = results[t]
        half = n // 2
        mine = (pos // 2) * side + lane
        same = pos % 2 == parity

        def one(d, carry):
            slot = (mine + d) % half
            target = (slot // side * 2 + parity) * side + slot % side
            pltpu.make_async_remote_copy(
                src_ref=source.at[h, rows(target), :],
                dst_ref=landing.at[:, columns(me, h)],
                send_sem=out_send.at[t, h],
                recv_sem=out_recv.at[t],
                device_id=to(target),
                device_id_type=MESH,
            ).start()
            return carry

        lax.fori_loop(jnp.where(same, 1, 0), half, one, 0)

        @pl.when(same)
        def _():
            pltpu.make_async_copy(
                source.at[h, rows(me), :], landing.at[:, columns(me, h)], out_recv.at[t]
            ).start()

    block = math.gcd(tokens, 256)

    def self_head(h):
        wait_in((0, 1, 2), h)
        attend(q_buf.at[h], k_buf.at[h], v_buf.at[h], None, so_buf.at[h], block)
        send_out(0, h, 0)
        send_out(0, h, 1)

    def hail(sem, line, lane_of):
        pl.semaphore_signal(
            sem, inc=1, device_id=to(line * side + lane_of), device_id_type=MESH
        )

    @pl.when(middle)
    def _():
        hail(barrier, low + high - pos, lane)
        pl.semaphore_wait(barrier, 1)

        @pl.when(pos == low)
        def _():
            forward_up(text_in, pos, 0)

        @pl.when(pos == high)
        def _():
            forward_down(text_in, pos, 0)

        for line in outer_lines:
            for k in range(side):
                hail(barrier, line, k)
        pl.semaphore_wait(barrier, len(outer_lines) * side)

        @pl.when(pos == low)
        def _():
            for line in outer_lines:
                if line < low:
                    hail(ready, line, lane)
            forward_down(text_in, pos, 0)

        @pl.when(pos == high)
        def _():
            for line in outer_lines:
                if line > high:
                    hail(ready, line, lane)
            forward_up(text_in, pos, 0)

    @pl.when(jnp.logical_not(middle))
    def _():
        pl.semaphore_wait(barrier, 2 * side)
        for line in (low, high):
            for k in range(side):
                hail(barrier, line, k)
        pl.semaphore_wait(ready, 1)
        forward_up(text_in, pos, 0)
        forward_down(text_in, pos, 0)

    forward_side(text_in, pos)
    send_in((0, 1, 2), 0)
    for copy in w_copies + small_copies:
        copy.start()
    for step in range(1, max(lines, heads)):
        if step < lines:
            relay(step)
        if step < heads:
            send_in((0, 1, 2), step)
        if step == lines - 1 or (step == heads - 1 and heads > lines):
            for h in range(heads):
                send_in((3,), h)
        if step <= heads:
            self_head(step - 1)
    for h in range(max(lines, heads) - 1, heads):
        self_head(h)

    text_wait(me)
    for line in range(lines):
        for k in range(1, side):
            text_wait(line * side + (lane + k) % side)
    for copy in w_copies + small_copies:
        copy.wait()

    text_rows = n * shard
    flat = text.reshape(text_rows, text.shape[2])
    tall = math.gcd(text_rows, 256)
    wide = math.gcd(wk.shape[1], 256)
    across = wk.shape[1] // wide

    def project(step, carry):
        r = pl.ds(pl.multiple_of((step // across) * tall, tall), tall)
        c = pl.ds(pl.multiple_of((step % across) * wide, wide), wide)
        tk[r, c] = jnp.dot(flat[r, :], wk[:, c], preferred_element_type=F32).astype(BF16)
        tv[r, c] = jnp.dot(flat[r, :], wv[:, c], preferred_element_type=F32).astype(BF16)
        return carry

    lax.fori_loop(0, (text_rows // tall) * across, project, 0)

    arrival = lax.broadcasted_iota(jnp.int32, bias.shape, 1)
    limit = jnp.zeros(bias.shape, jnp.int32)
    for j in range(n):
        held = length_ref[0] - block_ref[j] * shard
        limit = jnp.where(arrival // shard == j, held, limit)
    bias[...] = jnp.where(arrival % shard < limit, 0.0, -jnp.inf).astype(F32)

    for h in range(heads):
        c = slice(h * dim, (h + 1) * dim)
        wait_in((3,), h)
        attend(c_buf.at[h], tk.at[:, c], tv.at[:, c], bias, co_buf.at[h], block)
        send_out(1, h, 0)
        if h < heads - 4:
            send_out(1, h, 1)
    for h in range(max(heads - 4, 0), heads):
        send_out(1, h, 1)

    for t in range(4):
        landing = arrays[t][1]
        for h in range(heads):
            part = landing.at[h, pl.ds(0, (n - 1) * own), :]
            pltpu.make_async_copy(part, part, in_send.at[t, h]).wait()
    for t in range(2):
        source, landing = results[t]
        for h in range(heads):
            part = source.at[h, pl.ds(0, (n - 1) * own), :]
            pltpu.make_async_copy(part, part, out_send.at[t, h]).wait()
        pltpu.make_async_copy(landing, landing, out_recv.at[t]).wait()

    for step in range(lines):
        up = text_send(text_in, me, me, up_send.at[step])
        down = text_send(text_in, me, me, down_send.at[step])

        @pl.when(jnp.logical_and(pos + 1 < lines, pos >= step))
        def _():
            up.wait_send()

        @pl.when(jnp.logical_and(pos >= 1, pos + step < lines))
        def _():
            down.wait_send()

        for k in range(1, side):
            text_send(text_in, me, me, side_send.at[step, k]).wait_send()


def settle_kernel(a, b, a_out, b_out, sem):
    copies = [
        pltpu.make_async_copy(a, a_out, sem.at[0]),
        pltpu.make_async_copy(b, b_out, sem.at[1]),
    ]
    for copy in copies:
        copy.start()
    for copy in copies:
        copy.wait()


def settle(pair):
    any_spec = pl.BlockSpec(memory_space=pl.ANY)
    return tuple(
        pl.pallas_call(
            settle_kernel,
            name="settle",
            out_shape=[pltpu.HBM(x.shape, x.dtype) for x in pair],
            in_specs=[any_spec] * 2,
            out_specs=[any_spec] * 2,
            scratch_shapes=[pltpu.SemaphoreType.DMA((2,))],
            compiler_params=pltpu.CompilerParams(vmem_limit_bytes=1024 * 1024),
        )(*pair)
    )


def body(
    video_query,
    video_key,
    video_value,
    cross_query,
    text_rows,
    text_block,
    text_length,
    key_weight,
    value_weight,
):
    n = lax.axis_size("seq")
    lines = 4 if n % 4 == 0 else n
    own, inner = video_query.shape
    shard, d_text = text_rows.shape
    width = key_weight.shape[1]
    heads = width // HEAD_DIM
    tokens = own * n
    any_spec = pl.BlockSpec(memory_space=pl.ANY)
    head_buf = pltpu.VMEM((heads, tokens, HEAD_DIM), BF16)
    dma = pltpu.SemaphoreType.DMA
    return settle(
        pl.pallas_call(
            functools.partial(kernel, n, lines),
            name="video_block",
            out_shape=[pltpu.VMEM((own, inner), BF16)] * 2,
            in_specs=[any_spec] * 9,
            out_specs=[any_spec] * 2,
            scratch_shapes=[head_buf] * 6
            + [
                pltpu.VMEM((n, shard, d_text), BF16),
                pltpu.VMEM((d_text, width), BF16),
                pltpu.VMEM((d_text, width), BF16),
                pltpu.VMEM((n * shard, width), BF16),
                pltpu.VMEM((n * shard, width), BF16),
                pltpu.VMEM((1, n * shard), F32),
                pltpu.SMEM((n,), jnp.int32),
                pltpu.SMEM((1,), jnp.int32),
                dma((4, heads)),
                dma((4, heads)),
                dma((2, heads)),
                dma((2,)),
                dma((n,)),
                dma((lines,)),
                dma((lines,)),
                dma((lines, max(n // lines, 2))),
                dma((2,)),
                dma((2,)),
                pltpu.SemaphoreType.REGULAR,
            ],
            compiler_params=pltpu.CompilerParams(
                collective_id=0, has_side_effects=True, vmem_limit_bytes=58 * 1024 * 1024
            ),
        )(
            text_block,
            text_length,
            video_query,
            video_key,
            video_value,
            cross_query,
            text_rows,
            key_weight,
            value_weight,
        )
    )


def solution(mesh):
    return jax.shard_map(
        body,
        mesh=mesh,
        in_specs=(
            P(("clip", "seq"), None),
            P(("clip", "seq"), None),
            P(("clip", "seq"), None),
            P(("clip", "seq"), None),
            P(("clip", "seq"), None),
            P("clip"),
            P("clip"),
            P(None, "seq"),
            P(None, "seq"),
        ),
        out_specs=(P(("clip", "seq"), None), P(("clip", "seq"), None)),
        check_vma=False,
    )
```

```python
import functools
import math

import jax
import jax.numpy as jnp
from jax import lax
from jax.experimental import pallas as pl
from jax.experimental.pallas import tpu as pltpu
from jax.sharding import PartitionSpec as P

HEAD_DIM = 128
MESH = pl.DeviceIdType.MESH
F32 = jnp.float32
BF16 = jnp.bfloat16
SCORE_SCALE = HEAD_DIM ** (-0.5) * math.log2(math.e)


def softmax_rows(scores, bias):
    scores = scores * SCORE_SCALE
    if bias is not None:
        scores = scores + bias
    highest = jnp.max(scores, axis=-1, keepdims=True)
    exponent = jnp.exp2(scores - highest)
    total = jnp.sum(exponent, axis=-1, keepdims=True)
    return (exponent * (1.0 / total)).astype(BF16)


def attend(query, key, value, bias, out, block):
    def one(step, carry):
        rows = pl.ds(pl.multiple_of(step * block, block), block)
        scores = lax.dot_general(
            query[rows, :], key[...], (((1,), (1,)), ((), ())), preferred_element_type=F32
        )
        weights = softmax_rows(scores, None if bias is None else bias[...])
        out[rows, :] = jnp.dot(weights, value[...], preferred_element_type=F32).astype(BF16)
        return carry

    lax.fori_loop(0, query.shape[0] // block, one, 0)


def kernel(
    n,
    lines,
    block_in,
    length_in,
    q_in,
    k_in,
    v_in,
    c_in,
    text_in,
    wk_in,
    wv_in,
    self_out,
    cross_out,
    taken,
    made,
    text,
    weights,
    tk,
    tv,
    bias,
    block_ref,
    length_ref,
    in_send,
    qkv_recv,
    c_recv,
    out_send,
    out_recv,
    line_recv,
    side_recv,
    line_send,
    side_send,
    w_sem,
    small_sem,
    ready,
):
    heads, _, tokens, dim = taken.shape
    own = tokens // n
    shard = text.shape[1]
    me = lax.axis_index("seq")
    side = n // lines
    split = lines // 2
    low, high = split - 1, split
    outer_lines = [line for line in range(lines) if line not in (low, high)]
    pos = me // side
    lane = me % side
    middle = jnp.logical_or(pos == low, pos == high)

    def to(target):
        return {"seq": target}

    def far(target):
        return target // side // split != pos // split

    barrier = pltpu.get_barrier_semaphore()

    def hail(sem, line, lane_of):
        pl.semaphore_signal(
            sem, inc=1, device_id=to(line * side + lane_of), device_id_type=MESH
        )

    loads = [
        pltpu.make_async_copy(wk_in, weights.at[0], w_sem),
        pltpu.make_async_copy(wv_in, weights.at[1], w_sem),
        pltpu.make_async_copy(block_in, block_ref, small_sem.at[0]),
        pltpu.make_async_copy(length_in, length_ref, small_sem.at[1]),
    ]
    own_text = pltpu.make_async_copy(text_in, text.at[me], line_recv.at[pos])

    def text_send(source, index, target, sem, recv):
        return pltpu.make_async_remote_copy(
            src_ref=source,
            dst_ref=text.at[index],
            send_sem=sem,
            recv_sem=recv,
            device_id=to(target),
            device_id_type=MESH,
        )

    def forward_up(source, line):
        copy = text_send(source, line * side + lane, me + side, line_send, line_recv.at[line])

        @pl.when(pos + 1 < lines)
        def _():
            copy.start()

    def forward_down(source, line):
        copy = text_send(source, line * side + lane, me - side, line_send, line_recv.at[line])

        @pl.when(pos >= 1)
        def _():
            copy.start()

    def forward_side(source, line):
        for k in range(1, side):
            target = pos * side + (lane + k) % side
            text_send(source, line * side + lane, target, side_send, side_recv).start()

    def line_wait(line):
        shard_ref = text.at[line * side + lane]
        pltpu.make_async_copy(shard_ref, shard_ref, line_recv.at[line]).wait()

    def relay(step):
        @pl.when(pos >= step)
        def _():
            line = pos - step
            source = text.at[line * side + lane]
            line_wait(line)
            forward_up(source, line)
            forward_side(source, line)

        @pl.when(pos + step < lines)
        def _():
            line = pos + step
            source = text.at[line * side + lane]
            line_wait(line)
            forward_down(source, line)
            forward_side(source, line)

    sources = (q_in, k_in, v_in, c_in)

    def columns(owner, h):
        return pl.ds(pl.multiple_of((owner * heads + h) * dim, dim), dim)

    def rows(owner):
        return pl.ds(pl.multiple_of(owner * own, own), own)

    def send_in(which, h, recv):
        def one(d, carry):
            target = (me + d) % n
            for t in which:
                pltpu.make_async_remote_copy(
                    src_ref=sources[t].at[:, columns(target, h)],
                    dst_ref=taken.at[h, t, rows(me), :],
                    send_sem=in_send,
                    recv_sem=recv.at[h],
                    device_id=to(target),
                    device_id_type=MESH,
                ).start()
            return carry

        for t in which:
            pltpu.make_async_copy(
                sources[t].at[:, columns(me, h)], taken.at[h, t, rows(me), :], recv.at[h]
            ).start()
        lax.fori_loop(1, n, one, 0)

    results = (self_out, cross_out)

    def send_out(t, h, late):
        source, landing = made.at[t, h], results[t]

        def one(d, carry):
            target = (me + d) % n
            last = jnp.logical_and(far(target), target // side % 2 == 1)

            @pl.when(last if late else jnp.logical_not(last))
            def _():
                pltpu.make_async_remote_copy(
                    src_ref=source.at[rows(target), :],
                    dst_ref=landing.at[:, columns(me, h)],
                    send_sem=out_send,
                    recv_sem=out_recv.at[t],
                    device_id=to(target),
                    device_id_type=MESH,
                ).start()

            return carry

        lax.fori_loop(1, n, one, 0)
        if not late:
            pltpu.make_async_copy(
                source.at[rows(me), :], landing.at[:, columns(me, h)], out_recv.at[t]
            ).start()

    block = math.gcd(tokens, 256)

    def self_head(h):
        arrived = taken.at[h, pl.ds(0, 3)]
        pltpu.make_async_copy(arrived, arrived, qkv_recv.at[h]).wait()
        attend(taken.at[h, 0], taken.at[h, 1], taken.at[h, 2], None, made.at[0, h], block)
        send_out(0, h, False)
        send_out(0, h, True)

    @pl.when(middle)
    def _():
        hail(barrier, low + high - pos, lane)
        own_text.start()
        pl.semaphore_wait(barrier, 1)

        @pl.when(pos == low)
        def _():
            forward_up(text_in, pos)

        @pl.when(pos == high)
        def _():
            forward_down(text_in, pos)

        for line in outer_lines:
            for k in range(side):
                hail(barrier, line, k)
        pl.semaphore_wait(barrier, len(outer_lines) * side)

        @pl.when(pos == low)
        def _():
            for line in outer_lines:
                if line < low:
                    hail(ready, line, lane)
            forward_down(text_in, pos)

        @pl.when(pos == high)
        def _():
            for line in outer_lines:
                if line > high:
                    hail(ready, line, lane)
            forward_up(text_in, pos)

    @pl.when(jnp.logical_not(middle))
    def _():
        own_text.start()
        pl.semaphore_wait(barrier, 2 * side)
        for line in (low, high):
            for k in range(side):
                hail(barrier, line, k)
        pl.semaphore_wait(ready, 1)
        forward_up(text_in, pos)
        forward_down(text_in, pos)

    forward_side(text_in, pos)
    send_in((0, 1, 2), 0, qkv_recv)
    for copy in loads:
        copy.start()
    for step in range(1, max(lines, heads)):
        if step < lines:
            relay(step)
        if step < heads:
            send_in((0, 1, 2), step, qkv_recv)
        if step == lines - 1 or (step == heads - 1 and heads > lines):
            for h in range(heads):
                send_in((3,), h, c_recv)
        if step <= heads:
            self_head(step - 1)
    for h in range(max(lines, heads) - 1, heads):
        self_head(h)

    line_wait(pos)
    if side > 1:
        others = text.at[pl.ds(0, n - lines)]
        pltpu.make_async_copy(others, others, side_recv).wait()
    pltpu.make_async_copy(weights, weights, w_sem).wait()
    for copy in loads[2:]:
        copy.wait()

    text_rows = n * shard
    flat = text.reshape(text_rows, text.shape[2])
    width = weights.shape[2]
    tall = math.gcd(text_rows, 256)
    wide = math.gcd(width, 256)
    across = width // wide

    def project(step, carry):
        r = pl.ds(pl.multiple_of((step // across) * tall, tall), tall)
        c = pl.ds(pl.multiple_of((step % across) * wide, wide), wide)
        for which, out in ((0, tk), (1, tv)):
            out[r, c] = jnp.dot(
                flat[r, :], weights[which, :, c], preferred_element_type=F32
            ).astype(BF16)
        return carry

    lax.fori_loop(0, (text_rows // tall) * across, project, 0)

    arrival = lax.broadcasted_iota(jnp.int32, bias.shape, 1)
    limit = jnp.zeros(bias.shape, jnp.int32)
    for j in range(n):
        held = length_ref[0] - block_ref[j] * shard
        limit = jnp.where(arrival // shard == j, held, limit)
    bias[...] = jnp.where(arrival % shard < limit, 0.0, -jnp.inf).astype(F32)

    for h in range(heads):
        c = slice(h * dim, (h + 1) * dim)
        arrived = taken.at[h, 3]
        pltpu.make_async_copy(arrived, arrived, c_recv.at[h]).wait()
        attend(arrived, tk.at[:, c], tv.at[:, c], bias, made.at[1, h], block)
        send_out(1, h, False)
    for h in range(heads):
        send_out(1, h, True)

    away = pl.ds(0, (n - 1) * own)
    part = taken.at[:, :, away, :]
    pltpu.make_async_copy(part, part, in_send).wait()
    for p in range(lines):
        sent = (p + 1) * (p + 1 < lines) + (lines - p) * (p >= 1)

        @pl.when(pos == p)
        def _():
            part = text.at[pl.ds(0, sent)]
            pltpu.make_async_copy(part, part, line_send).wait()

    if side > 1:
        others = text.at[pl.ds(0, n - lines)]
        pltpu.make_async_copy(others, others, side_send).wait()
    part = made.at[:, :, away, :]
    pltpu.make_async_copy(part, part, out_send).wait()
    for t in range(2):
        pltpu.make_async_copy(results[t], results[t], out_recv.at[t]).wait()


def settle_kernel(a, b, a_out, b_out, sem):
    copies = [
        pltpu.make_async_copy(a, a_out, sem.at[0]),
        pltpu.make_async_copy(b, b_out, sem.at[1]),
    ]
    for copy in copies:
        copy.start()
    for copy in copies:
        copy.wait()


def settle(pair):
    any_spec = pl.BlockSpec(memory_space=pl.ANY)
    return tuple(
        pl.pallas_call(
            settle_kernel,
            name="settle",
            out_shape=[pltpu.HBM(x.shape, x.dtype) for x in pair],
            in_specs=[any_spec] * 2,
            out_specs=[any_spec] * 2,
            scratch_shapes=[pltpu.SemaphoreType.DMA((2,))],
            compiler_params=pltpu.CompilerParams(vmem_limit_bytes=1024 * 1024),
        )(*pair)
    )


def body(
    video_query,
    video_key,
    video_value,
    cross_query,
    text_rows,
    text_block,
    text_length,
    key_weight,
    value_weight,
):
    n = lax.axis_size("seq")
    lines = 4 if n % 4 == 0 else n
    own, inner = video_query.shape
    shard, d_text = text_rows.shape
    width = key_weight.shape[1]
    heads = width // HEAD_DIM
    tokens = own * n
    any_spec = pl.BlockSpec(memory_space=pl.ANY)
    dma = pltpu.SemaphoreType.DMA
    return settle(
        pl.pallas_call(
            functools.partial(kernel, n, lines),
            name="video_block",
            out_shape=[pltpu.VMEM((own, inner), BF16)] * 2,
            in_specs=[any_spec] * 9,
            out_specs=[any_spec] * 2,
            scratch_shapes=[
                pltpu.VMEM((heads, 4, tokens, HEAD_DIM), BF16),
                pltpu.VMEM((2, heads, tokens, HEAD_DIM), BF16),
                pltpu.VMEM((n, shard, d_text), BF16),
                pltpu.VMEM((2, d_text, width), BF16),
                pltpu.VMEM((n * shard, width), BF16),
                pltpu.VMEM((n * shard, width), BF16),
                pltpu.VMEM((1, n * shard), F32),
                pltpu.SMEM((n,), jnp.int32),
                pltpu.SMEM((1,), jnp.int32),
                dma(()),
                dma((heads,)),
                dma((heads,)),
                dma(()),
                dma((2,)),
                dma((lines,)),
                dma(()),
                dma(()),
                dma(()),
                dma(()),
                dma((2,)),
                pltpu.SemaphoreType.REGULAR,
            ],
            compiler_params=pltpu.CompilerParams(
                collective_id=0, has_side_effects=True, vmem_limit_bytes=58 * 1024 * 1024
            ),
        )(
            text_block,
            text_length,
            video_query,
            video_key,
            video_value,
            cross_query,
            text_rows,
            key_weight,
            value_weight,
        )
    )


def solution(mesh):
    return jax.shard_map(
        body,
        mesh=mesh,
        in_specs=(
            P(("clip", "seq"), None),
            P(("clip", "seq"), None),
            P(("clip", "seq"), None),
            P(("clip", "seq"), None),
            P(("clip", "seq"), None),
            P("clip"),
            P("clip"),
            P(None, "seq"),
            P(None, "seq"),
        ),
        out_specs=(P(("clip", "seq"), None), P(("clip", "seq"), None)),
        check_vma=False,
    )
```

```python
import functools
import math

import jax
import jax.numpy as jnp
from jax import lax
from jax.experimental import pallas as pl
from jax.experimental.pallas import tpu as pltpu
from jax.sharding import PartitionSpec as P

HEAD_DIM = 128
MESH = pl.DeviceIdType.MESH
F32 = jnp.float32
BF16 = jnp.bfloat16
SCORE_SCALE = HEAD_DIM ** (-0.5) * math.log2(math.e)


def softmax_rows(scores, bias):
    scores = scores * SCORE_SCALE
    if bias is not None:
        scores = scores + bias
    highest = jnp.max(scores, axis=-1, keepdims=True)
    exponent = jnp.exp2(scores - highest)
    total = jnp.sum(exponent, axis=-1, keepdims=True)
    return (exponent * (1.0 / total)).astype(BF16)


def attend(query, key, value, bias, out, block):
    def one(step, carry):
        rows = pl.ds(pl.multiple_of(step * block, block), block)
        scores = lax.dot_general(
            query[rows, :], key[...], (((1,), (1,)), ((), ())), preferred_element_type=F32
        )
        weights = softmax_rows(scores, None if bias is None else bias[...])
        out[rows, :] = jnp.dot(weights, value[...], preferred_element_type=F32).astype(BF16)
        return carry

    lax.fori_loop(0, query.shape[0] // block, one, 0)


def kernel(
    n,
    lines,
    block_in,
    length_in,
    q_in,
    k_in,
    v_in,
    c_in,
    text_in,
    wk_in,
    wv_in,
    self_out,
    cross_out,
    taken,
    made,
    text,
    weights,
    tk,
    tv,
    bias,
    block_ref,
    length_ref,
    in_send,
    qkv_recv,
    c_recv,
    out_send,
    out_recv,
    line_recv,
    side_recv,
    line_send,
    side_send,
    w_sem,
    small_sem,
    ready,
):
    heads, _, tokens, dim = taken.shape
    own = tokens // n
    shard = text.shape[1]
    me = lax.axis_index("seq")
    side = n // lines
    split = lines // 2
    low, high = split - 1, split
    outer_lines = [line for line in range(lines) if line not in (low, high)]
    pos = me // side
    lane = me % side
    middle = jnp.logical_or(pos == low, pos == high)

    def to(target):
        return {"seq": target}

    def far(target):
        return target // side // split != pos // split

    barrier = pltpu.get_barrier_semaphore()

    def hail(sem, line, lane_of):
        pl.semaphore_signal(
            sem, inc=1, device_id=to(line * side + lane_of), device_id_type=MESH
        )

    loads = [
        pltpu.make_async_copy(wk_in, weights.at[0], w_sem),
        pltpu.make_async_copy(wv_in, weights.at[1], w_sem),
        pltpu.make_async_copy(block_in, block_ref, small_sem.at[0]),
        pltpu.make_async_copy(length_in, length_ref, small_sem.at[1]),
    ]
    own_text = pltpu.make_async_copy(text_in, text.at[me], line_recv.at[pos])

    def text_send(source, index, target, sem, recv):
        return pltpu.make_async_remote_copy(
            src_ref=source,
            dst_ref=text.at[index],
            send_sem=sem,
            recv_sem=recv,
            device_id=to(target),
            device_id_type=MESH,
        )

    def forward_up(source, line):
        copy = text_send(source, line * side + lane, me + side, line_send, line_recv.at[line])

        @pl.when(pos + 1 < lines)
        def _():
            copy.start()

    def forward_down(source, line):
        copy = text_send(source, line * side + lane, me - side, line_send, line_recv.at[line])

        @pl.when(pos >= 1)
        def _():
            copy.start()

    def forward_side(source, line):
        for k in range(1, side):
            target = pos * side + (lane + k) % side
            text_send(source, line * side + lane, target, side_send, side_recv).start()

    def line_wait(line):
        shard_ref = text.at[line * side + lane]
        pltpu.make_async_copy(shard_ref, shard_ref, line_recv.at[line]).wait()

    def relay(step):
        @pl.when(pos >= step)
        def _():
            line = pos - step
            source = text.at[line * side + lane]
            line_wait(line)
            forward_up(source, line)
            forward_side(source, line)

        @pl.when(pos + step < lines)
        def _():
            line = pos + step
            source = text.at[line * side + lane]
            line_wait(line)
            forward_down(source, line)
            forward_side(source, line)

    sources = (q_in, k_in, v_in, c_in)

    def columns(owner, h):
        return pl.ds(pl.multiple_of((owner * heads + h) * dim, dim), dim)

    def rows(owner):
        return pl.ds(pl.multiple_of(owner * own, own), own)

    def send_in(which, h, recv):
        def one(d, carry):
            target = (me + d) % n
            for t in which:
                pltpu.make_async_remote_copy(
                    src_ref=sources[t].at[:, columns(target, h)],
                    dst_ref=taken.at[h, t, rows(me), :],
                    send_sem=in_send,
                    recv_sem=recv.at[h],
                    device_id=to(target),
                    device_id_type=MESH,
                ).start()
            return carry

        for t in which:
            pltpu.make_async_copy(
                sources[t].at[:, columns(me, h)], taken.at[h, t, rows(me), :], recv.at[h]
            ).start()
        lax.fori_loop(1, n, one, 0)

    results = (self_out, cross_out)

    def send_out(t, h, stages):
        source, landing = made.at[t, h], results[t]

        def one(d, carry):
            target = (me + d) % n
            stage = jnp.where(far(target), target // side % split + target % side, 0)
            now = functools.reduce(jnp.logical_or, [stage == k for k in stages])

            @pl.when(now)
            def _():
                pltpu.make_async_remote_copy(
                    src_ref=source.at[rows(target), :],
                    dst_ref=landing.at[:, columns(me, h)],
                    send_sem=out_send,
                    recv_sem=out_recv.at[t],
                    device_id=to(target),
                    device_id_type=MESH,
                ).start()

            return carry

        lax.fori_loop(1, n, one, 0)
        if 0 in stages:
            pltpu.make_async_copy(
                source.at[rows(me), :], landing.at[:, columns(me, h)], out_recv.at[t]
            ).start()

    block = math.gcd(tokens, 256)
    stages = split + side - 1

    def self_head(h):
        arrived = taken.at[h, pl.ds(0, 3)]
        pltpu.make_async_copy(arrived, arrived, qkv_recv.at[h]).wait()
        attend(taken.at[h, 0], taken.at[h, 1], taken.at[h, 2], None, made.at[0, h], block)
        for stage in range(stages):
            send_out(0, h, (stage,))

    @pl.when(middle)
    def _():
        hail(barrier, low + high - pos, lane)
        own_text.start()
        pl.semaphore_wait(barrier, 1)

        @pl.when(pos == low)
        def _():
            forward_up(text_in, pos)

        @pl.when(pos == high)
        def _():
            forward_down(text_in, pos)

        for line in outer_lines:
            for k in range(side):
                hail(barrier, line, k)
        pl.semaphore_wait(barrier, len(outer_lines) * side)

        @pl.when(pos == low)
        def _():
            for line in outer_lines:
                if line < low:
                    hail(ready, line, lane)
            forward_down(text_in, pos)

        @pl.when(pos == high)
        def _():
            for line in outer_lines:
                if line > high:
                    hail(ready, line, lane)
            forward_up(text_in, pos)

    @pl.when(jnp.logical_not(middle))
    def _():
        own_text.start()
        pl.semaphore_wait(barrier, 2 * side)
        for line in (low, high):
            for k in range(side):
                hail(barrier, line, k)
        pl.semaphore_wait(ready, 1)
        forward_up(text_in, pos)
        forward_down(text_in, pos)

    forward_side(text_in, pos)
    send_in((0, 1, 2), 0, qkv_recv)
    for copy in loads:
        copy.start()
    for step in range(1, max(lines, heads)):
        if step < lines:
            relay(step)
        if step < heads:
            send_in((0, 1, 2), step, qkv_recv)
        if step == lines - 1 or (step == heads - 1 and heads > lines):
            for h in range(heads):
                send_in((3,), h, c_recv)
        if step <= heads:
            self_head(step - 1)
    for h in range(max(lines, heads) - 1, heads):
        self_head(h)

    line_wait(pos)
    if side > 1:
        others = text.at[pl.ds(0, n - lines)]
        pltpu.make_async_copy(others, others, side_recv).wait()
    pltpu.make_async_copy(weights, weights, w_sem).wait()
    for copy in loads[2:]:
        copy.wait()

    text_rows = n * shard
    flat = text.reshape(text_rows, text.shape[2])
    width = weights.shape[2]
    tall = math.gcd(text_rows, 256)
    wide = math.gcd(width, 256)
    across = width // wide

    def project(step, carry):
        r = pl.ds(pl.multiple_of((step // across) * tall, tall), tall)
        c = pl.ds(pl.multiple_of((step % across) * wide, wide), wide)
        for which, out in ((0, tk), (1, tv)):
            out[r, c] = jnp.dot(
                flat[r, :], weights[which, :, c], preferred_element_type=F32
            ).astype(BF16)
        return carry

    lax.fori_loop(0, (text_rows // tall) * across, project, 0)

    arrival = lax.broadcasted_iota(jnp.int32, bias.shape, 1)
    limit = jnp.zeros(bias.shape, jnp.int32)
    for j in range(n):
        held = length_ref[0] - block_ref[j] * shard
        limit = jnp.where(arrival // shard == j, held, limit)
    bias[...] = jnp.where(arrival % shard < limit, 0.0, -jnp.inf).astype(F32)

    for h in range(heads):
        c = slice(h * dim, (h + 1) * dim)
        arrived = taken.at[h, 3]
        pltpu.make_async_copy(arrived, arrived, c_recv.at[h]).wait()
        attend(arrived, tk.at[:, c], tv.at[:, c], bias, made.at[1, h], block)
        send_out(1, h, (0,))
    for stage in range(1, stages):
        for h in range(heads):
            send_out(1, h, (stage,))

    away = pl.ds(0, (n - 1) * own)
    part = taken.at[:, :, away, :]
    pltpu.make_async_copy(part, part, in_send).wait()
    for p in range(lines):
        sent = (p + 1) * (p + 1 < lines) + (lines - p) * (p >= 1)

        @pl.when(pos == p)
        def _():
            part = text.at[pl.ds(0, sent)]
            pltpu.make_async_copy(part, part, line_send).wait()

    if side > 1:
        others = text.at[pl.ds(0, n - lines)]
        pltpu.make_async_copy(others, others, side_send).wait()
    part = made.at[:, :, away, :]
    pltpu.make_async_copy(part, part, out_send).wait()
    for t in range(2):
        pltpu.make_async_copy(results[t], results[t], out_recv.at[t]).wait()


def settle_kernel(a, b, a_out, b_out, sem):
    copies = [
        pltpu.make_async_copy(a, a_out, sem.at[0]),
        pltpu.make_async_copy(b, b_out, sem.at[1]),
    ]
    for copy in copies:
        copy.start()
    for copy in copies:
        copy.wait()


def settle(pair):
    any_spec = pl.BlockSpec(memory_space=pl.ANY)
    return tuple(
        pl.pallas_call(
            settle_kernel,
            name="settle",
            out_shape=[pltpu.HBM(x.shape, x.dtype) for x in pair],
            in_specs=[any_spec] * 2,
            out_specs=[any_spec] * 2,
            scratch_shapes=[pltpu.SemaphoreType.DMA((2,))],
            compiler_params=pltpu.CompilerParams(vmem_limit_bytes=1024 * 1024),
        )(*pair)
    )


def body(
    video_query,
    video_key,
    video_value,
    cross_query,
    text_rows,
    text_block,
    text_length,
    key_weight,
    value_weight,
):
    n = lax.axis_size("seq")
    lines = 4 if n % 4 == 0 else n
    own, inner = video_query.shape
    shard, d_text = text_rows.shape
    width = key_weight.shape[1]
    heads = width // HEAD_DIM
    tokens = own * n
    any_spec = pl.BlockSpec(memory_space=pl.ANY)
    dma = pltpu.SemaphoreType.DMA
    return settle(
        pl.pallas_call(
            functools.partial(kernel, n, lines),
            name="video_block",
            out_shape=[pltpu.VMEM((own, inner), BF16)] * 2,
            in_specs=[any_spec] * 9,
            out_specs=[any_spec] * 2,
            scratch_shapes=[
                pltpu.VMEM((heads, 4, tokens, HEAD_DIM), BF16),
                pltpu.VMEM((2, heads, tokens, HEAD_DIM), BF16),
                pltpu.VMEM((n, shard, d_text), BF16),
                pltpu.VMEM((2, d_text, width), BF16),
                pltpu.VMEM((n * shard, width), BF16),
                pltpu.VMEM((n * shard, width), BF16),
                pltpu.VMEM((1, n * shard), F32),
                pltpu.SMEM((n,), jnp.int32),
                pltpu.SMEM((1,), jnp.int32),
                dma(()),
                dma((heads,)),
                dma((heads,)),
                dma(()),
                dma((2,)),
                dma((lines,)),
                dma(()),
                dma(()),
                dma(()),
                dma(()),
                dma((2,)),
                pltpu.SemaphoreType.REGULAR,
            ],
            compiler_params=pltpu.CompilerParams(
                collective_id=0, has_side_effects=True, vmem_limit_bytes=58 * 1024 * 1024
            ),
        )(
            text_block,
            text_length,
            video_query,
            video_key,
            video_value,
            cross_query,
            text_rows,
            key_weight,
            value_weight,
        )
    )


def solution(mesh):
    return jax.shard_map(
        body,
        mesh=mesh,
        in_specs=(
            P(("clip", "seq"), None),
            P(("clip", "seq"), None),
            P(("clip", "seq"), None),
            P(("clip", "seq"), None),
            P(("clip", "seq"), None),
            P("clip"),
            P("clip"),
            P(None, "seq"),
            P(None, "seq"),
        ),
        out_specs=(P(("clip", "seq"), None), P(("clip", "seq"), None)),
        check_vma=False,
    )
```

```python
import functools
import math

import jax
import jax.numpy as jnp
from jax import lax
from jax.experimental import pallas as pl
from jax.experimental.pallas import tpu as pltpu
from jax.sharding import PartitionSpec as P

HEAD_DIM = 128
MESH = pl.DeviceIdType.MESH
F32 = jnp.float32
BF16 = jnp.bfloat16
SCORE_SCALE = HEAD_DIM ** (-0.5) * math.log2(math.e)


def softmax_rows(scores, bias):
    scores = scores * SCORE_SCALE
    if bias is not None:
        scores = scores + bias
    highest = jnp.max(scores, axis=-1, keepdims=True)
    exponent = jnp.exp2(scores - highest)
    total = jnp.sum(exponent, axis=-1, keepdims=True)
    return (exponent * (1.0 / total)).astype(BF16)


def attend(query, key, value, bias, out, block):
    def one(step, carry):
        rows = pl.ds(pl.multiple_of(step * block, block), block)
        scores = lax.dot_general(
            query[rows, :], key[...], (((1,), (1,)), ((), ())), preferred_element_type=F32
        )
        weights = softmax_rows(scores, None if bias is None else bias[...])
        out[rows, :] = jnp.dot(weights, value[...], preferred_element_type=F32).astype(BF16)
        return carry

    lax.fori_loop(0, query.shape[0] // block, one, 0)


def kernel(
    n,
    lines,
    block_in,
    length_in,
    q_in,
    k_in,
    v_in,
    c_in,
    text_in,
    wk_in,
    wv_in,
    self_out,
    cross_out,
    taken,
    made,
    text,
    weights,
    tk,
    tv,
    bias,
    block_ref,
    length_ref,
    in_send,
    qkv_recv,
    c_recv,
    out_send,
    out_recv,
    line_recv,
    side_recv,
    line_send,
    side_send,
    w_sem,
    small_sem,
    ready,
):
    heads, _, tokens, dim = taken.shape
    own = tokens // n
    shard = text.shape[1]
    me = lax.axis_index("seq")
    side = n // lines
    split = lines // 2
    low, high = split - 1, split
    outer_lines = [line for line in range(lines) if line not in (low, high)]
    pos = me // side
    lane = me % side
    middle = jnp.logical_or(pos == low, pos == high)

    def to(target):
        return {"seq": target}

    def far(target):
        return target // side // split != pos // split

    barrier = pltpu.get_barrier_semaphore()

    def hail(sem, line, lane_of):
        pl.semaphore_signal(
            sem, inc=1, device_id=to(line * side + lane_of), device_id_type=MESH
        )

    loads = [
        pltpu.make_async_copy(wk_in, weights.at[0], w_sem),
        pltpu.make_async_copy(wv_in, weights.at[1], w_sem),
        pltpu.make_async_copy(block_in, block_ref, small_sem.at[0]),
        pltpu.make_async_copy(length_in, length_ref, small_sem.at[1]),
    ]
    own_text = pltpu.make_async_copy(text_in, text.at[me], line_recv.at[pos])

    def text_send(source, index, target, sem, recv):
        return pltpu.make_async_remote_copy(
            src_ref=source,
            dst_ref=text.at[index],
            send_sem=sem,
            recv_sem=recv,
            device_id=to(target),
            device_id_type=MESH,
        )

    def forward_up(source, line):
        copy = text_send(source, line * side + lane, me + side, line_send, line_recv.at[line])

        @pl.when(pos + 1 < lines)
        def _():
            copy.start()

    def forward_down(source, line):
        copy = text_send(source, line * side + lane, me - side, line_send, line_recv.at[line])

        @pl.when(pos >= 1)
        def _():
            copy.start()

    def forward_side(source, line):
        for k in range(1, side):
            target = pos * side + (lane + k) % side
            text_send(source, line * side + lane, target, side_send, side_recv).start()

    def line_wait(line):
        shard_ref = text.at[line * side + lane]
        pltpu.make_async_copy(shard_ref, shard_ref, line_recv.at[line]).wait()

    def relay(step):
        @pl.when(pos >= step)
        def _():
            line = pos - step
            source = text.at[line * side + lane]
            line_wait(line)
            forward_up(source, line)
            forward_side(source, line)

        @pl.when(pos + step < lines)
        def _():
            line = pos + step
            source = text.at[line * side + lane]
            line_wait(line)
            forward_down(source, line)
            forward_side(source, line)

    sources = (q_in, k_in, v_in, c_in)

    def columns(owner, h):
        return pl.ds(pl.multiple_of((owner * heads + h) * dim, dim), dim)

    def rows(owner):
        return pl.ds(pl.multiple_of(owner * own, own), own)

    def send_in(which, h, recv):
        def one(d, carry):
            target = (me + d) % n
            for t in which:
                pltpu.make_async_remote_copy(
                    src_ref=sources[t].at[:, columns(target, h)],
                    dst_ref=taken.at[h, t, rows(me), :],
                    send_sem=in_send,
                    recv_sem=recv.at[h],
                    device_id=to(target),
                    device_id_type=MESH,
                ).start()
            return carry

        for t in which:
            pltpu.make_async_copy(
                sources[t].at[:, columns(me, h)], taken.at[h, t, rows(me), :], recv.at[h]
            ).start()
        lax.fori_loop(1, n, one, 0)

    results = (self_out, cross_out)

    def send_out(t, h, stages):
        source, landing = made.at[t, h], results[t]

        def one(d, carry):
            target = (me + d) % n
            stage = jnp.where(far(target), target // side % split + target % side, 0)
            now = functools.reduce(jnp.logical_or, [stage == k for k in stages])

            @pl.when(now)
            def _():
                pltpu.make_async_remote_copy(
                    src_ref=source.at[rows(target), :],
                    dst_ref=landing.at[:, columns(me, h)],
                    send_sem=out_send,
                    recv_sem=out_recv.at[t],
                    device_id=to(target),
                    device_id_type=MESH,
                ).start()

            return carry

        lax.fori_loop(1, n, one, 0)
        if 0 in stages:
            pltpu.make_async_copy(
                source.at[rows(me), :], landing.at[:, columns(me, h)], out_recv.at[t]
            ).start()

    block = math.gcd(tokens, 256)
    stages = split + side - 1

    def self_head(h):
        arrived = taken.at[h, pl.ds(0, 3)]
        pltpu.make_async_copy(arrived, arrived, qkv_recv.at[h]).wait()
        attend(taken.at[h, 0], taken.at[h, 1], taken.at[h, 2], None, made.at[0, h], block)
        send_out(0, h, range(stages))

    @pl.when(middle)
    def _():
        hail(barrier, low + high - pos, lane)
        own_text.start()

        @pl.when(pos == low)
        def _():
            line_wait(pos)

        pl.semaphore_wait(barrier, 1)

        @pl.when(pos == low)
        def _():
            forward_up(text.at[me], pos)

        @pl.when(pos == high)
        def _():
            forward_down(text_in, pos)

        for line in outer_lines:
            for k in range(side):
                hail(barrier, line, k)
        pl.semaphore_wait(barrier, len(outer_lines) * side)

        @pl.when(pos == low)
        def _():
            for line in outer_lines:
                if line < low:
                    hail(ready, line, lane)
            forward_down(text_in, pos)

        @pl.when(pos == high)
        def _():
            for line in outer_lines:
                if line > high:
                    hail(ready, line, lane)
            forward_up(text_in, pos)

    @pl.when(jnp.logical_not(middle))
    def _():
        own_text.start()
        pl.semaphore_wait(barrier, 2 * side)
        for line in (low, high):
            for k in range(side):
                hail(barrier, line, k)
        pl.semaphore_wait(ready, 1)
        forward_up(text_in, pos)
        forward_down(text_in, pos)

    forward_side(text_in, pos)
    send_in((0, 1, 2), 0, qkv_recv)
    for copy in loads:
        copy.start()
    for step in range(1, max(lines, heads)):
        if step < lines:
            relay(step)
        if step < heads:
            send_in((0, 1, 2), step, qkv_recv)
        if step == lines - 1 or (step == heads - 1 and heads > lines):
            for h in range(heads):
                send_in((3,), h, c_recv)
        if step <= heads:
            self_head(step - 1)
    for h in range(max(lines, heads) - 1, heads):
        self_head(h)

    @pl.when(pos != low)
    def _():
        line_wait(pos)

    if side > 1:
        others = text.at[pl.ds(0, n - lines)]
        pltpu.make_async_copy(others, others, side_recv).wait()
    pltpu.make_async_copy(weights, weights, w_sem).wait()
    for copy in loads[2:]:
        copy.wait()

    text_rows = n * shard
    flat = text.reshape(text_rows, text.shape[2])
    width = weights.shape[2]
    tall = math.gcd(text_rows, 256)
    wide = math.gcd(width, 256)
    across = width // wide

    def project(step, carry):
        r = pl.ds(pl.multiple_of((step // across) * tall, tall), tall)
        c = pl.ds(pl.multiple_of((step % across) * wide, wide), wide)
        for which, out in ((0, tk), (1, tv)):
            out[r, c] = jnp.dot(
                flat[r, :], weights[which, :, c], preferred_element_type=F32
            ).astype(BF16)
        return carry

    lax.fori_loop(0, (text_rows // tall) * across, project, 0)

    arrival = lax.broadcasted_iota(jnp.int32, bias.shape, 1)
    limit = jnp.zeros(bias.shape, jnp.int32)
    for j in range(n):
        held = length_ref[0] - block_ref[j] * shard
        limit = jnp.where(arrival // shard == j, held, limit)
    bias[...] = jnp.where(arrival % shard < limit, 0.0, -jnp.inf).astype(F32)

    for h in range(heads):
        c = slice(h * dim, (h + 1) * dim)
        arrived = taken.at[h, 3]
        pltpu.make_async_copy(arrived, arrived, c_recv.at[h]).wait()
        attend(arrived, tk.at[:, c], tv.at[:, c], bias, made.at[1, h], block)
        send_out(1, h, (0,))
    for stage in range(1, stages):
        for h in range(heads):
            send_out(1, h, (stage,))

    away = pl.ds(0, (n - 1) * own)
    part = taken.at[:, :, away, :]
    pltpu.make_async_copy(part, part, in_send).wait()
    for p in range(lines):
        sent = (p + 1) * (p + 1 < lines) + (lines - p) * (p >= 1)

        @pl.when(pos == p)
        def _():
            part = text.at[pl.ds(0, sent)]
            pltpu.make_async_copy(part, part, line_send).wait()

    if side > 1:
        others = text.at[pl.ds(0, n - lines)]
        pltpu.make_async_copy(others, others, side_send).wait()
    part = made.at[:, :, away, :]
    pltpu.make_async_copy(part, part, out_send).wait()
    for t in range(2):
        pltpu.make_async_copy(results[t], results[t], out_recv.at[t]).wait()


def settle_kernel(a, b, a_out, b_out, sem):
    copies = [
        pltpu.make_async_copy(a, a_out, sem.at[0]),
        pltpu.make_async_copy(b, b_out, sem.at[1]),
    ]
    for copy in copies:
        copy.start()
    for copy in copies:
        copy.wait()


def settle(pair):
    any_spec = pl.BlockSpec(memory_space=pl.ANY)
    return tuple(
        pl.pallas_call(
            settle_kernel,
            name="settle",
            out_shape=[pltpu.HBM(x.shape, x.dtype) for x in pair],
            in_specs=[any_spec] * 2,
            out_specs=[any_spec] * 2,
            scratch_shapes=[pltpu.SemaphoreType.DMA((2,))],
            compiler_params=pltpu.CompilerParams(vmem_limit_bytes=1024 * 1024),
        )(*pair)
    )


def body(
    video_query,
    video_key,
    video_value,
    cross_query,
    text_rows,
    text_block,
    text_length,
    key_weight,
    value_weight,
):
    n = lax.axis_size("seq")
    lines = 4 if n % 4 == 0 else n
    own, inner = video_query.shape
    shard, d_text = text_rows.shape
    width = key_weight.shape[1]
    heads = width // HEAD_DIM
    tokens = own * n
    any_spec = pl.BlockSpec(memory_space=pl.ANY)
    dma = pltpu.SemaphoreType.DMA
    return settle(
        pl.pallas_call(
            functools.partial(kernel, n, lines),
            name="video_block",
            out_shape=[pltpu.VMEM((own, inner), BF16)] * 2,
            in_specs=[any_spec] * 9,
            out_specs=[any_spec] * 2,
            scratch_shapes=[
                pltpu.VMEM((heads, 4, tokens, HEAD_DIM), BF16),
                pltpu.VMEM((2, heads, tokens, HEAD_DIM), BF16),
                pltpu.VMEM((n, shard, d_text), BF16),
                pltpu.VMEM((2, d_text, width), BF16),
                pltpu.VMEM((n * shard, width), BF16),
                pltpu.VMEM((n * shard, width), BF16),
                pltpu.VMEM((1, n * shard), F32),
                pltpu.SMEM((n,), jnp.int32),
                pltpu.SMEM((1,), jnp.int32),
                dma(()),
                dma((heads,)),
                dma((heads,)),
                dma(()),
                dma((2,)),
                dma((lines,)),
                dma(()),
                dma(()),
                dma(()),
                dma(()),
                dma((2,)),
                pltpu.SemaphoreType.REGULAR,
            ],
            compiler_params=pltpu.CompilerParams(
                collective_id=0, has_side_effects=True, vmem_limit_bytes=58 * 1024 * 1024
            ),
        )(
            text_block,
            text_length,
            video_query,
            video_key,
            video_value,
            cross_query,
            text_rows,
            key_weight,
            value_weight,
        )
    )


def solution(mesh):
    return jax.shard_map(
        body,
        mesh=mesh,
        in_specs=(
            P(("clip", "seq"), None),
            P(("clip", "seq"), None),
            P(("clip", "seq"), None),
            P(("clip", "seq"), None),
            P(("clip", "seq"), None),
            P("clip"),
            P("clip"),
            P(None, "seq"),
            P(None, "seq"),
        ),
        out_specs=(P(("clip", "seq"), None), P(("clip", "seq"), None)),
        check_vma=False,
    )
```

```python
import functools
import math

import jax
import jax.numpy as jnp
from jax import lax
from jax.experimental import pallas as pl
from jax.experimental.pallas import tpu as pltpu
from jax.sharding import PartitionSpec as P

HEAD_DIM = 128
MESH = pl.DeviceIdType.MESH
F32 = jnp.float32
BF16 = jnp.bfloat16
SCORE_SCALE = HEAD_DIM ** (-0.5) * math.log2(math.e)


def softmax_rows(scores, bias):
    scores = scores * SCORE_SCALE
    if bias is not None:
        scores = scores + bias
    highest = jnp.max(scores, axis=-1, keepdims=True)
    exponent = jnp.exp2(scores - highest)
    total = jnp.sum(exponent, axis=-1, keepdims=True)
    return (exponent * (1.0 / total)).astype(BF16)


def attend(query, key, value, bias, out, block):
    def one(step, carry):
        rows = pl.ds(pl.multiple_of(step * block, block), block)
        scores = lax.dot_general(
            query[rows, :], key[...], (((1,), (1,)), ((), ())), preferred_element_type=F32
        )
        weights = softmax_rows(scores, None if bias is None else bias[...])
        out[rows, :] = jnp.dot(weights, value[...], preferred_element_type=F32).astype(BF16)
        return carry

    lax.fori_loop(0, query.shape[0] // block, one, 0)


def kernel(
    n,
    lines,
    block_in,
    length_in,
    q_in,
    k_in,
    v_in,
    c_in,
    text_in,
    wk_in,
    wv_in,
    self_out,
    cross_out,
    taken,
    made,
    text,
    weights,
    tk,
    tv,
    bias,
    block_ref,
    length_ref,
    in_send,
    qkv_recv,
    c_recv,
    out_send,
    out_recv,
    line_recv,
    side_recv,
    line_send,
    side_send,
    w_sem,
    small_sem,
    ready,
):
    heads, _, tokens, dim = taken.shape
    own = tokens // n
    shard = text.shape[1]
    me = lax.axis_index("seq")
    side = n // lines
    split = lines // 2
    low, high = split - 1, split
    outer_lines = [line for line in range(lines) if line not in (low, high)]
    pos = me // side
    lane = me % side
    middle = jnp.logical_or(pos == low, pos == high)

    def to(target):
        return {"seq": target}

    def far(target):
        return target // side // split != pos // split

    barrier = pltpu.get_barrier_semaphore()

    def hail(sem, line, lane_of):
        pl.semaphore_signal(
            sem, inc=1, device_id=to(line * side + lane_of), device_id_type=MESH
        )

    loads = [
        pltpu.make_async_copy(wk_in, weights.at[0], w_sem),
        pltpu.make_async_copy(wv_in, weights.at[1], w_sem),
        pltpu.make_async_copy(block_in, block_ref, small_sem.at[0]),
        pltpu.make_async_copy(length_in, length_ref, small_sem.at[1]),
    ]
    own_text = pltpu.make_async_copy(text_in, text.at[me], line_recv.at[pos])

    def text_send(source, index, target, sem, recv):
        return pltpu.make_async_remote_copy(
            src_ref=source,
            dst_ref=text.at[index],
            send_sem=sem,
            recv_sem=recv,
            device_id=to(target),
            device_id_type=MESH,
        )

    def forward_up(source, line):
        copy = text_send(source, line * side + lane, me + side, line_send, line_recv.at[line])

        @pl.when(pos + 1 < lines)
        def _():
            copy.start()

    def forward_down(source, line):
        copy = text_send(source, line * side + lane, me - side, line_send, line_recv.at[line])

        @pl.when(pos >= 1)
        def _():
            copy.start()

    def forward_side(source, line):
        for k in range(1, side):
            target = pos * side + (lane + k) % side
            text_send(source, line * side + lane, target, side_send, side_recv).start()

    def line_wait(line):
        shard_ref = text.at[line * side + lane]
        pltpu.make_async_copy(shard_ref, shard_ref, line_recv.at[line]).wait()

    def relay(step):
        @pl.when(pos >= step)
        def _():
            line = pos - step
            source = text.at[line * side + lane]
            line_wait(line)
            forward_up(source, line)
            forward_side(source, line)

        @pl.when(pos + step < lines)
        def _():
            line = pos + step
            source = text.at[line * side + lane]
            line_wait(line)
            forward_down(source, line)
            forward_side(source, line)

    sources = (q_in, k_in, v_in, c_in)

    def columns(owner, h):
        return pl.ds(pl.multiple_of((owner * heads + h) * dim, dim), dim)

    def rows(owner):
        return pl.ds(pl.multiple_of(owner * own, own), own)

    def send_in(which, h, recv):
        def one(d, carry):
            target = (me + d) % n
            for t in which:
                pltpu.make_async_remote_copy(
                    src_ref=sources[t].at[:, columns(target, h)],
                    dst_ref=taken.at[h, t, rows(me), :],
                    send_sem=in_send,
                    recv_sem=recv.at[h],
                    device_id=to(target),
                    device_id_type=MESH,
                ).start()
            return carry

        for t in which:
            pltpu.make_async_copy(
                sources[t].at[:, columns(me, h)], taken.at[h, t, rows(me), :], recv.at[h]
            ).start()
        lax.fori_loop(1, n, one, 0)

    results = (self_out, cross_out)

    def send_out(t, h, stages):
        source, landing = made.at[t, h], results[t]

        def one(d, carry):
            target = (me + d) % n
            stage = jnp.where(far(target), target // side % split + target % side, 0)
            now = functools.reduce(jnp.logical_or, [stage == k for k in stages])

            @pl.when(now)
            def _():
                pltpu.make_async_remote_copy(
                    src_ref=source.at[rows(target), :],
                    dst_ref=landing.at[:, columns(me, h)],
                    send_sem=out_send,
                    recv_sem=out_recv.at[t],
                    device_id=to(target),
                    device_id_type=MESH,
                ).start()

            return carry

        lax.fori_loop(1, n, one, 0)
        if 0 in stages:
            pltpu.make_async_copy(
                source.at[rows(me), :], landing.at[:, columns(me, h)], out_recv.at[t]
            ).start()

    block = math.gcd(tokens, 256)
    stages = split + side - 1

    def self_head(h):
        arrived = taken.at[h, pl.ds(0, 3)]
        pltpu.make_async_copy(arrived, arrived, qkv_recv.at[h]).wait()
        attend(taken.at[h, 0], taken.at[h, 1], taken.at[h, 2], None, made.at[0, h], block)
        send_out(0, h, range(stages))

    @pl.when(middle)
    def _():
        hail(barrier, low + high - pos, lane)
        own_text.start()

        @pl.when(pos == low)
        def _():
            line_wait(pos)

        pl.semaphore_wait(barrier, 1)

        @pl.when(pos == low)
        def _():
            forward_up(text.at[me], pos)

        @pl.when(pos == high)
        def _():
            forward_down(text_in, pos)

        for line in outer_lines:
            for k in range(side):
                hail(barrier, line, k)
        pl.semaphore_wait(barrier, len(outer_lines) * side)

        @pl.when(pos == low)
        def _():
            for line in outer_lines:
                if line < low:
                    hail(ready, line, lane)
            forward_down(text_in, pos)

        @pl.when(pos == high)
        def _():
            for line in outer_lines:
                if line > high:
                    hail(ready, line, lane)
            forward_up(text_in, pos)

    @pl.when(jnp.logical_not(middle))
    def _():
        own_text.start()
        pl.semaphore_wait(barrier, 2 * side)
        for line in (low, high):
            for k in range(side):
                hail(barrier, line, k)
        pl.semaphore_wait(ready, 1)
        forward_up(text_in, pos)
        forward_down(text_in, pos)

    forward_side(text_in, pos)
    send_in((0, 1, 2), 0, qkv_recv)
    for copy in loads:
        copy.start()
    for step in range(1, max(lines, heads)):
        if step < lines:
            relay(step)
        if step < heads:
            send_in((0, 1, 2), step, qkv_recv)
        if step == lines - 1 or (step == heads - 1 and heads > lines):
            for h in range(heads):
                send_in((3,), h, c_recv)
        if step <= heads:
            self_head(step - 1)
    for h in range(max(lines, heads) - 1, heads):
        self_head(h)

    @pl.when(pos != low)
    def _():
        line_wait(pos)

    if side > 1:
        others = text.at[pl.ds(0, n - lines)]
        pltpu.make_async_copy(others, others, side_recv).wait()
    pltpu.make_async_copy(weights, weights, w_sem).wait()
    for copy in loads[2:]:
        copy.wait()

    text_rows = n * shard
    flat = text.reshape(text_rows, text.shape[2])
    width = weights.shape[2]
    tall = math.gcd(text_rows, 256)
    wide = math.gcd(width, 256)
    across = width // wide

    def project(step, carry):
        r = pl.ds(pl.multiple_of((step // across) * tall, tall), tall)
        c = pl.ds(pl.multiple_of((step % across) * wide, wide), wide)
        for which, out in ((0, tk), (1, tv)):
            out[r, c] = jnp.dot(
                flat[r, :], weights[which, :, c], preferred_element_type=F32
            ).astype(BF16)
        return carry

    lax.fori_loop(0, (text_rows // tall) * across, project, 0)

    arrival = lax.broadcasted_iota(jnp.int32, bias.shape, 1)
    limit = jnp.zeros(bias.shape, jnp.int32)
    for j in range(n):
        held = length_ref[0] - block_ref[j] * shard
        limit = jnp.where(arrival // shard == j, held, limit)
    bias[...] = jnp.where(arrival % shard < limit, 0.0, -jnp.inf).astype(F32)

    for h in range(heads):
        c = slice(h * dim, (h + 1) * dim)
        arrived = taken.at[h, 3]
        pltpu.make_async_copy(arrived, arrived, c_recv.at[h]).wait()
        attend(arrived, tk.at[:, c], tv.at[:, c], bias, made.at[1, h], block)
        send_out(1, h, (0,))
    for step in range(heads + stages):
        for stage in range(1, stages):
            h = step - 2 * (stage - 1)
            if 0 <= h < heads:
                send_out(1, h, (stage,))

    away = pl.ds(0, (n - 1) * own)
    part = taken.at[:, :, away, :]
    pltpu.make_async_copy(part, part, in_send).wait()
    for p in range(lines):
        sent = (p + 1) * (p + 1 < lines) + (lines - p) * (p >= 1)

        @pl.when(pos == p)
        def _():
            part = text.at[pl.ds(0, sent)]
            pltpu.make_async_copy(part, part, line_send).wait()

    if side > 1:
        others = text.at[pl.ds(0, n - lines)]
        pltpu.make_async_copy(others, others, side_send).wait()
    part = made.at[:, :, away, :]
    pltpu.make_async_copy(part, part, out_send).wait()
    for t in range(2):
        pltpu.make_async_copy(results[t], results[t], out_recv.at[t]).wait()


def settle_kernel(a, b, a_out, b_out, sem):
    copies = [
        pltpu.make_async_copy(a, a_out, sem.at[0]),
        pltpu.make_async_copy(b, b_out, sem.at[1]),
    ]
    for copy in copies:
        copy.start()
    for copy in copies:
        copy.wait()


def settle(pair):
    any_spec = pl.BlockSpec(memory_space=pl.ANY)
    return tuple(
        pl.pallas_call(
            settle_kernel,
            name="settle",
            out_shape=[pltpu.HBM(x.shape, x.dtype) for x in pair],
            in_specs=[any_spec] * 2,
            out_specs=[any_spec] * 2,
            scratch_shapes=[pltpu.SemaphoreType.DMA((2,))],
            compiler_params=pltpu.CompilerParams(vmem_limit_bytes=1024 * 1024),
        )(*pair)
    )


def body(
    video_query,
    video_key,
    video_value,
    cross_query,
    text_rows,
    text_block,
    text_length,
    key_weight,
    value_weight,
):
    n = lax.axis_size("seq")
    lines = 4 if n % 4 == 0 else n
    own, inner = video_query.shape
    shard, d_text = text_rows.shape
    width = key_weight.shape[1]
    heads = width // HEAD_DIM
    tokens = own * n
    any_spec = pl.BlockSpec(memory_space=pl.ANY)
    dma = pltpu.SemaphoreType.DMA
    return settle(
        pl.pallas_call(
            functools.partial(kernel, n, lines),
            name="video_block",
            out_shape=[pltpu.VMEM((own, inner), BF16)] * 2,
            in_specs=[any_spec] * 9,
            out_specs=[any_spec] * 2,
            scratch_shapes=[
                pltpu.VMEM((heads, 4, tokens, HEAD_DIM), BF16),
                pltpu.VMEM((2, heads, tokens, HEAD_DIM), BF16),
                pltpu.VMEM((n, shard, d_text), BF16),
                pltpu.VMEM((2, d_text, width), BF16),
                pltpu.VMEM((n * shard, width), BF16),
                pltpu.VMEM((n * shard, width), BF16),
                pltpu.VMEM((1, n * shard), F32),
                pltpu.SMEM((n,), jnp.int32),
                pltpu.SMEM((1,), jnp.int32),
                dma(()),
                dma((heads,)),
                dma((heads,)),
                dma(()),
                dma((2,)),
                dma((lines,)),
                dma(()),
                dma(()),
                dma(()),
                dma(()),
                dma((2,)),
                pltpu.SemaphoreType.REGULAR,
            ],
            compiler_params=pltpu.CompilerParams(
                collective_id=0, has_side_effects=True, vmem_limit_bytes=58 * 1024 * 1024
            ),
        )(
            text_block,
            text_length,
            video_query,
            video_key,
            video_value,
            cross_query,
            text_rows,
            key_weight,
            value_weight,
        )
    )


def solution(mesh):
    return jax.shard_map(
        body,
        mesh=mesh,
        in_specs=(
            P(("clip", "seq"), None),
            P(("clip", "seq"), None),
            P(("clip", "seq"), None),
            P(("clip", "seq"), None),
            P(("clip", "seq"), None),
            P("clip"),
            P("clip"),
            P(None, "seq"),
            P(None, "seq"),
        ),
        out_specs=(P(("clip", "seq"), None), P(("clip", "seq"), None)),
        check_vma=False,
    )
```

```python
import functools
import math

import jax
import jax.numpy as jnp
from jax import lax
from jax.experimental import pallas as pl
from jax.experimental.pallas import tpu as pltpu
from jax.sharding import PartitionSpec as P

HEAD_DIM = 128
MESH = pl.DeviceIdType.MESH
F32 = jnp.float32
BF16 = jnp.bfloat16
SCORE_SCALE = HEAD_DIM ** (-0.5) * math.log2(math.e)


def softmax_rows(scores, bias):
    scores = scores * SCORE_SCALE
    if bias is not None:
        scores = scores + bias
    highest = jnp.max(scores, axis=-1, keepdims=True)
    exponent = jnp.exp2(scores - highest)
    total = jnp.sum(exponent, axis=-1, keepdims=True)
    return (exponent * (1.0 / total)).astype(BF16)


def attend(query, key, value, bias, out, block):
    def one(step, carry):
        rows = pl.ds(pl.multiple_of(step * block, block), block)
        scores = lax.dot_general(
            query[rows, :], key[...], (((1,), (1,)), ((), ())), preferred_element_type=F32
        )
        weights = softmax_rows(scores, None if bias is None else bias[...])
        out[rows, :] = jnp.dot(weights, value[...], preferred_element_type=F32).astype(BF16)
        return carry

    lax.fori_loop(0, query.shape[0] // block, one, 0)


def kernel(
    n,
    lines,
    block_in,
    length_in,
    q_in,
    k_in,
    v_in,
    c_in,
    text_in,
    wk_in,
    wv_in,
    self_out,
    cross_out,
    taken,
    made,
    text,
    weights,
    tk,
    tv,
    bias,
    block_ref,
    length_ref,
    in_send,
    qkv_recv,
    c_recv,
    out_send,
    out_recv,
    line_recv,
    side_recv,
    line_send,
    side_send,
    w_sem,
    small_sem,
    ready,
):
    heads, _, tokens, dim = taken.shape
    own = tokens // n
    shard = text.shape[1]
    me = lax.axis_index("seq")
    side = n // lines
    split = lines // 2
    low, high = split - 1, split
    outer_lines = [line for line in range(lines) if line not in (low, high)]
    pos = me // side
    lane = me % side
    middle = jnp.logical_or(pos == low, pos == high)

    def to(target):
        return {"seq": target}

    def far(target):
        return target // side // split != pos // split

    barrier = pltpu.get_barrier_semaphore()

    def hail(sem, line, lane_of):
        pl.semaphore_signal(
            sem, inc=1, device_id=to(line * side + lane_of), device_id_type=MESH
        )

    loads = [
        pltpu.make_async_copy(wk_in, weights.at[0], w_sem),
        pltpu.make_async_copy(wv_in, weights.at[1], w_sem),
        pltpu.make_async_copy(block_in, block_ref, small_sem.at[0]),
        pltpu.make_async_copy(length_in, length_ref, small_sem.at[1]),
    ]
    own_text = pltpu.make_async_copy(text_in, text.at[me], line_recv.at[pos])

    def text_send(source, index, target, sem, recv):
        return pltpu.make_async_remote_copy(
            src_ref=source,
            dst_ref=text.at[index],
            send_sem=sem,
            recv_sem=recv,
            device_id=to(target),
            device_id_type=MESH,
        )

    def forward_up(source, line):
        copy = text_send(source, line * side + lane, me + side, line_send, line_recv.at[line])

        @pl.when(pos + 1 < lines)
        def _():
            copy.start()

    def forward_down(source, line):
        copy = text_send(source, line * side + lane, me - side, line_send, line_recv.at[line])

        @pl.when(pos >= 1)
        def _():
            copy.start()

    def forward_side(source, line):
        for k in range(1, side):
            target = pos * side + (lane + k) % side
            text_send(source, line * side + lane, target, side_send, side_recv).start()

    def line_wait(line):
        shard_ref = text.at[line * side + lane]
        pltpu.make_async_copy(shard_ref, shard_ref, line_recv.at[line]).wait()

    def relay(step):
        @pl.when(pos >= step)
        def _():
            line = pos - step
            source = text.at[line * side + lane]
            line_wait(line)
            forward_up(source, line)
            forward_side(source, line)

        @pl.when(pos + step < lines)
        def _():
            line = pos + step
            source = text.at[line * side + lane]
            line_wait(line)
            forward_down(source, line)
            forward_side(source, line)

    sources = (q_in, k_in, v_in, c_in)

    def columns(owner, h):
        return pl.ds(pl.multiple_of((owner * heads + h) * dim, dim), dim)

    def rows(owner):
        return pl.ds(pl.multiple_of(owner * own, own), own)

    ahead = jnp.logical_and(pos == low, lane != 0)

    def send_block(which, h, recv, target):
        for t in which:
            pltpu.make_async_remote_copy(
                src_ref=sources[t].at[:, columns(target, h)],
                dst_ref=taken.at[h, t, rows(me), :],
                send_sem=in_send,
                recv_sem=recv.at[h],
                device_id=to(target),
                device_id_type=MESH,
            ).start()

    def send_in(which, h, recv, held=False):
        def one(d, carry):
            target = (me + d) % n
            sent = jnp.logical_and(held, target == high * side)

            @pl.when(jnp.logical_not(sent))
            def _():
                send_block(which, h, recv, target)

            return carry

        for t in which:
            pltpu.make_async_copy(
                sources[t].at[:, columns(me, h)], taken.at[h, t, rows(me), :], recv.at[h]
            ).start()
        lax.fori_loop(1, n, one, 0)

    results = (self_out, cross_out)

    def send_out(t, h, stages):
        source, landing = made.at[t, h], results[t]

        def one(d, carry):
            target = (me + d) % n
            stage = jnp.where(far(target), target // side % split + target % side, 0)
            now = functools.reduce(jnp.logical_or, [stage == k for k in stages])

            @pl.when(now)
            def _():
                pltpu.make_async_remote_copy(
                    src_ref=source.at[rows(target), :],
                    dst_ref=landing.at[:, columns(me, h)],
                    send_sem=out_send,
                    recv_sem=out_recv.at[t],
                    device_id=to(target),
                    device_id_type=MESH,
                ).start()

            return carry

        lax.fori_loop(1, n, one, 0)
        if 0 in stages:
            pltpu.make_async_copy(
                source.at[rows(me), :], landing.at[:, columns(me, h)], out_recv.at[t]
            ).start()

    block = math.gcd(tokens, 256)
    stages = split + side - 1

    def self_head(h):
        arrived = taken.at[h, pl.ds(0, 3)]
        pltpu.make_async_copy(arrived, arrived, qkv_recv.at[h]).wait()
        attend(taken.at[h, 0], taken.at[h, 1], taken.at[h, 2], None, made.at[0, h], block)
        send_out(0, h, range(stages))

    @pl.when(middle)
    def _():
        @pl.when(pos == low)
        def _():
            hail(barrier, high, lane)

        @pl.when(jnp.logical_and(pos == high, lane == 0))
        def _():
            for k in range(side):
                hail(barrier, low, k)

        own_text.start()

        @pl.when(pos == low)
        def _():
            line_wait(pos)

        pl.semaphore_wait(barrier, 1)

        @pl.when(jnp.logical_and(pos == high, lane != 0))
        def _():
            hail(ready, low, lane)

        @pl.when(ahead)
        def _():
            send_block((0, 1, 2), 0, qkv_recv, high * side)
            pl.semaphore_wait(ready, 1)

        @pl.when(pos == low)
        def _():
            forward_up(text.at[me], pos)

        @pl.when(pos == high)
        def _():
            forward_down(text_in, pos)

        for line in outer_lines:
            for k in range(side):
                hail(barrier, line, k)
        pl.semaphore_wait(barrier, len(outer_lines) * side)

        @pl.when(pos == low)
        def _():
            for line in outer_lines:
                if line < low:
                    hail(ready, line, lane)
            forward_down(text_in, pos)

        @pl.when(pos == high)
        def _():
            for line in outer_lines:
                if line > high:
                    hail(ready, line, lane)
            forward_up(text_in, pos)

    @pl.when(jnp.logical_not(middle))
    def _():
        own_text.start()
        pl.semaphore_wait(barrier, 2 * side)
        for line in (low, high):
            for k in range(side):
                hail(barrier, line, k)
        pl.semaphore_wait(ready, 1)
        forward_up(text_in, pos)
        forward_down(text_in, pos)

    forward_side(text_in, pos)
    send_in((0, 1, 2), 0, qkv_recv, ahead)
    for copy in loads:
        copy.start()
    for step in range(1, max(lines, heads)):
        if step < lines:
            relay(step)
        if step < heads:
            send_in((0, 1, 2), step, qkv_recv)
        if step == lines - 1 or (step == heads - 1 and heads > lines):
            for h in range(heads):
                send_in((3,), h, c_recv)
        if step <= heads:
            self_head(step - 1)
    for h in range(max(lines, heads) - 1, heads):
        self_head(h)

    @pl.when(pos != low)
    def _():
        line_wait(pos)

    if side > 1:
        others = text.at[pl.ds(0, n - lines)]
        pltpu.make_async_copy(others, others, side_recv).wait()
    pltpu.make_async_copy(weights, weights, w_sem).wait()
    for copy in loads[2:]:
        copy.wait()

    text_rows = n * shard
    flat = text.reshape(text_rows, text.shape[2])
    width = weights.shape[2]
    tall = math.gcd(text_rows, 256)
    wide = math.gcd(width, 256)
    across = width // wide

    def project(step, carry):
        r = pl.ds(pl.multiple_of((step // across) * tall, tall), tall)
        c = pl.ds(pl.multiple_of((step % across) * wide, wide), wide)
        for which, out in ((0, tk), (1, tv)):
            out[r, c] = jnp.dot(
                flat[r, :], weights[which, :, c], preferred_element_type=F32
            ).astype(BF16)
        return carry

    lax.fori_loop(0, (text_rows // tall) * across, project, 0)

    arrival = lax.broadcasted_iota(jnp.int32, bias.shape, 1)
    limit = jnp.zeros(bias.shape, jnp.int32)
    for j in range(n):
        held = length_ref[0] - block_ref[j] * shard
        limit = jnp.where(arrival // shard == j, held, limit)
    bias[...] = jnp.where(arrival % shard < limit, 0.0, -jnp.inf).astype(F32)

    for h in range(heads):
        c = slice(h * dim, (h + 1) * dim)
        arrived = taken.at[h, 3]
        pltpu.make_async_copy(arrived, arrived, c_recv.at[h]).wait()
        attend(arrived, tk.at[:, c], tv.at[:, c], bias, made.at[1, h], block)
        send_out(1, h, (0,))
    for step in range(heads + stages):
        for stage in range(1, stages):
            h = step - 2 * (stage - 1)
            if 0 <= h < heads:
                send_out(1, h, (stage,))

    away = pl.ds(0, (n - 1) * own)
    part = taken.at[:, :, away, :]
    pltpu.make_async_copy(part, part, in_send).wait()
    for p in range(lines):
        sent = (p + 1) * (p + 1 < lines) + (lines - p) * (p >= 1)

        @pl.when(pos == p)
        def _():
            part = text.at[pl.ds(0, sent)]
            pltpu.make_async_copy(part, part, line_send).wait()

    if side > 1:
        others = text.at[pl.ds(0, n - lines)]
        pltpu.make_async_copy(others, others, side_send).wait()
    part = made.at[:, :, away, :]
    pltpu.make_async_copy(part, part, out_send).wait()
    for t in range(2):
        pltpu.make_async_copy(results[t], results[t], out_recv.at[t]).wait()


def settle_kernel(a, b, a_out, b_out, sem):
    copies = [
        pltpu.make_async_copy(a, a_out, sem.at[0]),
        pltpu.make_async_copy(b, b_out, sem.at[1]),
    ]
    for copy in copies:
        copy.start()
    for copy in copies:
        copy.wait()


def settle(pair):
    any_spec = pl.BlockSpec(memory_space=pl.ANY)
    return tuple(
        pl.pallas_call(
            settle_kernel,
            name="settle",
            out_shape=[pltpu.HBM(x.shape, x.dtype) for x in pair],
            in_specs=[any_spec] * 2,
            out_specs=[any_spec] * 2,
            scratch_shapes=[pltpu.SemaphoreType.DMA((2,))],
            compiler_params=pltpu.CompilerParams(vmem_limit_bytes=1024 * 1024),
        )(*pair)
    )


def body(
    video_query,
    video_key,
    video_value,
    cross_query,
    text_rows,
    text_block,
    text_length,
    key_weight,
    value_weight,
):
    n = lax.axis_size("seq")
    lines = 4 if n % 4 == 0 else n
    own, inner = video_query.shape
    shard, d_text = text_rows.shape
    width = key_weight.shape[1]
    heads = width // HEAD_DIM
    tokens = own * n
    any_spec = pl.BlockSpec(memory_space=pl.ANY)
    dma = pltpu.SemaphoreType.DMA
    return settle(
        pl.pallas_call(
            functools.partial(kernel, n, lines),
            name="video_block",
            out_shape=[pltpu.VMEM((own, inner), BF16)] * 2,
            in_specs=[any_spec] * 9,
            out_specs=[any_spec] * 2,
            scratch_shapes=[
                pltpu.VMEM((heads, 4, tokens, HEAD_DIM), BF16),
                pltpu.VMEM((2, heads, tokens, HEAD_DIM), BF16),
                pltpu.VMEM((n, shard, d_text), BF16),
                pltpu.VMEM((2, d_text, width), BF16),
                pltpu.VMEM((n * shard, width), BF16),
                pltpu.VMEM((n * shard, width), BF16),
                pltpu.VMEM((1, n * shard), F32),
                pltpu.SMEM((n,), jnp.int32),
                pltpu.SMEM((1,), jnp.int32),
                dma(()),
                dma((heads,)),
                dma((heads,)),
                dma(()),
                dma((2,)),
                dma((lines,)),
                dma(()),
                dma(()),
                dma(()),
                dma(()),
                dma((2,)),
                pltpu.SemaphoreType.REGULAR,
            ],
            compiler_params=pltpu.CompilerParams(
                collective_id=0, has_side_effects=True, vmem_limit_bytes=58 * 1024 * 1024
            ),
        )(
            text_block,
            text_length,
            video_query,
            video_key,
            video_value,
            cross_query,
            text_rows,
            key_weight,
            value_weight,
        )
    )


def solution(mesh):
    return jax.shard_map(
        body,
        mesh=mesh,
        in_specs=(
            P(("clip", "seq"), None),
            P(("clip", "seq"), None),
            P(("clip", "seq"), None),
            P(("clip", "seq"), None),
            P(("clip", "seq"), None),
            P("clip"),
            P("clip"),
            P(None, "seq"),
            P(None, "seq"),
        ),
        out_specs=(P(("clip", "seq"), None), P(("clip", "seq"), None)),
        check_vma=False,
    )
```
